32 devices in a mesh: seq: 16 (over z, x, core), head: 2 (over y).
Axes of the slice: x: 2, y: 2, z: 4, core: 2. Of those that a mesh axis runs over, the one named last changes fastest.
Arguments:
- sparse_query: bfloat16 [4096, 8192], P('seq', 'head'), may hold values from -62 to 62
- sparse_key: bfloat16 [4096, 1024], P('seq', 'head'), may hold values from -5 to 5
- sparse_value: bfloat16 [4096, 1024], P('seq', 'head'), may hold values from -5 to 5
- light_query: bfloat16 [4096, 8192], P('seq', 'head'), may hold values from -60 to 60
- light_key: bfloat16 [4096, 8192], P('seq', 'head'), may hold values from -0.5 to 0.5
- log_decay: float32 [64, 4096], P('head', 'seq'), may hold values from -1 to 0
- segments: int32 [4096], P('seq'), may hold values from 0 to 3, never falling along the last dimension, each value on 1 to 2048 neighbouring positions
- block_list: int32 [32, 12], P('seq'), may hold values from -1 to 29, as said below
Outputs:
- sparse_out: bfloat16 [4096, 8192], P('seq', 'head')
- mixed_out: bfloat16 [4096, 8192], P('seq', 'head')
The draws below stay inside these ranges and needn't reach their ends.
Inputs may be any that keep to these rules, and one draw needn't show every extreme that they name: `block_list`: entry -1 names no block. Every other entry of row b names a block of an earlier aligned group of 256 tokens than the group that holds block b; the rows of one aligned group of 256 tokens together name at most one block of any other group, and name it at most once. Some row names 12 blocks. `segments`: document ids may be packed several to a wider word wherever they travel.
All inputs are finite; a program needn't handle non-finite values.
Results may differ from the reference program's by a relative error of at most 0.0057.
Values may be sent and summed in bfloat16 or wider, within the bound.
No kernel may reach another device: no remote copies, remote signals or barrier semaphores. Data moves between devices by JAX's collectives and lax.ppermute only.
A program may use at most 128 MiB of HBM per device.

```python
import math
import jax
import jax.numpy as jnp
import numpy as np
from jax import lax

ASKER_CHANNELS = 64
HD = 128
KVH = 8
BLK = 128
KMAX = 12
TOK_DEV = 256
SEQUENCE_LENGTH = 4096
QBLK = 32


def paired_draw(key):
    base_key = jax.random.fold_in(key, 11)
    key_one, key_two = jax.random.split(base_key, 2)
    key_rows = jnp.clip(jax.random.normal(key_one, (SEQUENCE_LENGTH, KVH, HD), jnp.float32), -5.0, 5.0)
    query_rows = jnp.clip(jax.random.normal(key_two, (SEQUENCE_LENGTH, ASKER_CHANNELS, HD), jnp.float32), -5.0, 5.0)
    return (query_rows.reshape(SEQUENCE_LENGTH, ASKER_CHANNELS * HD), key_rows.reshape(SEQUENCE_LENGTH, KVH * HD))


def draw_sparse_query(key, part):
    return paired_draw(key)[0].astype(jnp.bfloat16)


def draw_sparse_key(key, part):
    return paired_draw(key)[1].astype(jnp.bfloat16)


def draw_light_query(key, part):
    key_one = jax.random.fold_in(jax.random.fold_in(key, 31), 0)
    head_index = jnp.arange(ASKER_CHANNELS * HD) // HD
    rising = 1.0 + 2.0 * head_index.astype(jnp.float32) / max(ASKER_CHANNELS - 1, 1)
    drawn = jnp.clip(jax.random.normal(key_one, (SEQUENCE_LENGTH, ASKER_CHANNELS * HD), jnp.float32), -5.0, 5.0) * rising[None, :]
    return drawn.astype(jnp.bfloat16)


def draw_log_decay(key, part):
    split_sampler_seeds = jax.random.split(jax.random.fold_in(key, 23), 6)
    fast_share = 0.5
    fast_low = 1.1 / TOK_DEV
    fast_high = min(8.0 / TOK_DEV, 0.15)
    fast_heads = jax.random.uniform(split_sampler_seeds[0], (ASKER_CHANNELS, 1), jnp.float32) < fast_share
    slow_rate = jnp.exp(jax.random.uniform(split_sampler_seeds[1], (ASKER_CHANNELS, 1), jnp.float32, math.log(0.05), math.log(0.5))) / SEQUENCE_LENGTH
    fast_rate = jnp.exp(jax.random.uniform(split_sampler_seeds[2], (ASKER_CHANNELS, 1), jnp.float32, math.log(fast_low), math.log(fast_high)))
    channel_fading_speed = jnp.where(fast_heads, fast_rate, slow_rate)
    sawtooth_magnitude = jnp.exp(jax.random.uniform(split_sampler_seeds[3], (ASKER_CHANNELS, SEQUENCE_LENGTH), jnp.float32, -math.log(2.0), math.log(2.0)))
    spike_location = jax.random.randint(split_sampler_seeds[4], (1, SEQUENCE_LENGTH), 0, max(SEQUENCE_LENGTH // 2, 1)) == 0
    spike_deduction = jnp.log(jax.random.uniform(split_sampler_seeds[5], (ASKER_CHANNELS, SEQUENCE_LENGTH), jnp.float32, 0.5, 0.8))
    drawn = -channel_fading_speed * sawtooth_magnitude + jnp.where(spike_location, spike_deduction, 0.0)
    return jnp.maximum(drawn, -1.0)


def draw_block_list(key, part):
    per_group = TOK_DEV // BLK
    shard_count = QBLK // per_group
    slot_count = per_group * KMAX
    top_count = min(slot_count, shard_count)
    split_sampler_seeds = jax.random.split(jax.random.fold_in(key, 41), 2)
    device_rows = jnp.arange(shard_count)[:, None]
    owner_cols = jnp.arange(shard_count)[None, :]
    owner_score = jax.random.randint(split_sampler_seeds[0], (shard_count, shard_count), 0, 1 << 16) * shard_count + owner_cols
    forced = (device_rows == shard_count - 1) & (owner_cols == shard_count - 2)
    owner_score = owner_score + jnp.where(forced, 1 << 28, 0)
    owner_score = jnp.where(owner_cols < device_rows, owner_score, -1)
    top_values, owners = lax.top_k(owner_score, top_count)
    valid = top_values >= 0
    chosen_half = jax.random.randint(split_sampler_seeds[1], (shard_count, top_count), 0, per_group)
    first_slot = (device_rows == shard_count - 1) & (jnp.arange(top_count)[None, :] == 0)
    chosen_half = jnp.where(first_slot, per_group - 1, chosen_half)
    named_block = jnp.where(valid, owners * per_group + chosen_half, -1)
    padding = jnp.full((shard_count, slot_count - top_count), -1, jnp.int32)
    listed = jnp.concatenate([named_block.astype(jnp.int32), padding], axis=1)
    return listed.reshape(QBLK, KMAX).astype(jnp.int32)


def block_scale(key, extent, pieces, least, largest):
    level = 1.0
    for axis_at, parts in pieces:
        steps = jax.random.uniform(jax.random.fold_in(jax.random.fold_in(key, 6), axis_at), (parts,), jnp.float32, least / len(pieces), largest / len(pieces))
        level = level * jnp.repeat(jnp.exp(steps), extent[axis_at] // parts).reshape((-1,) + (1,) * (len(extent) - 1 - axis_at))
    return level


def length_profile(count, total, bound, slope):
    loads = [(1 << 20) // math.isqrt(grade ** slope) + 1 for grade in range(2, count + 1)]
    spare, given = total - bound - (count - 1), [1] * (count - 1)
    while spare > 0:
        movable = [i for i in range(count - 1) if given[i] < bound]
        pool, budget = sum([loads[i] for i in movable]), spare
        for i in movable:
            extra = min(bound - given[i], max(1, budget * loads[i] // pool), spare)
            given[i] = given[i] + extra
            spare = spare - extra
    return np.array([bound] + given)


def ragged_sizes(key, amount, total, most, lean):
    if amount == 2:
        one = jax.random.randint(key, (), max(1, total - most), min(most, total - 1) + 1)
        return jnp.stack([one, total - one])
    sizes = jnp.asarray(length_profile(amount, total, most, lean), jnp.int32)
    pairs = (amount - 1) // 2
    donor, sink = sizes[1:1 + 2 * pairs:2], sizes[2:2 + 2 * pairs:2]
    slack = jnp.minimum(donor - 1, most - sink)
    shifted = jax.random.randint(jax.random.fold_in(key, 1), (pairs,), 0, 1 << 20) % (slack + 1)
    sizes = sizes.at[1:1 + 2 * pairs:2].set(donor - shifted).at[2:2 + 2 * pairs:2].set(sink + shifted)
    return sizes[jax.random.permutation(jax.random.fold_in(key, 2), amount)]


def noise(own_key, extent, scale, limit, cuts=(), kind=jnp.bfloat16):
    factor_of = block_scale(own_key, extent, cuts, -0.22, 0.18) if cuts else 1.0
    values = jax.random.normal(own_key, extent, jnp.float32) * scale * factor_of
    return jnp.minimum(jnp.maximum(values, -limit), limit).astype(kind)


def setup_inputs(seed: int = 0) -> dict:
    seeds = jax.random.split(jax.random.key(seed), 9)
    sparse_query = draw_sparse_query(jax.random.fold_in(seeds[8], 71), 0)
    sparse_key = draw_sparse_key(jax.random.fold_in(seeds[8], 71), 0)
    sparse_value = noise(seeds[2], (SEQUENCE_LENGTH, KVH * HD), 1.0, 5.0, ((0, 16), (1, 2)))
    light_query = draw_light_query(jax.random.fold_in(seeds[8], 71), 0)
    light_key = noise(seeds[4], (SEQUENCE_LENGTH, ASKER_CHANNELS * HD), HD ** -0.5, 0.5, ((0, 16), (1, 2)))
    log_decay = draw_log_decay(jax.random.fold_in(seeds[8], 71), 0)
    segments = jnp.searchsorted(jnp.cumsum(ragged_sizes(seeds[6], 4, SEQUENCE_LENGTH, SEQUENCE_LENGTH // 2, 1)), jnp.arange(SEQUENCE_LENGTH), side="right").astype(jnp.int32)
    block_list = draw_block_list(jax.random.fold_in(seeds[8], 71), 0)
    return {"sparse_query": sparse_query, "sparse_key": sparse_key, "sparse_value": sparse_value, "light_query": light_query, "light_key": light_key, "log_decay": log_decay, "segments": segments, "block_list": block_list}


big_negative = -1e+30
norm_eps = 1e-06

def attend_block(query, own_kv, own_seg, picked_kv, picked_seg, picked_ok):
    row_count = query.shape[0]
    kv_width = own_kv.shape[1] // 2
    kv_heads = kv_width // HD
    group_size = query.shape[1] // kv_width
    list_count = picked_kv.shape[0]
    keys_all = jnp.concatenate([own_kv, picked_kv.reshape(list_count * row_count, 2 * kv_width)], axis=0).astype(jnp.float32)
    seg_all = jnp.concatenate([own_seg, picked_seg.reshape(list_count * row_count)])
    queries = query.astype(jnp.float32).reshape(row_count, kv_heads, group_size, HD)
    key_part = keys_all[:, :kv_width].reshape(-1, kv_heads, HD)
    value_part = keys_all[:, kv_width:].reshape(-1, kv_heads, HD)
    scores = jnp.einsum('qkgd,nkd->kgqn', queries, key_part) * HD ** (-0.5)
    places = jnp.arange(row_count)
    causal = places[None, :] <= places[:, None]
    listed_ok = jnp.broadcast_to(jnp.repeat(picked_ok, row_count)[None, :], (row_count, list_count * row_count))
    allowed = jnp.concatenate([causal, listed_ok], axis=1) & (seg_all[None, :] == own_seg[:, None])
    scores = jnp.where(allowed[None, None], scores, big_negative)
    highest = lax.optimization_barrier(jnp.max(scores, axis=-1, keepdims=True))
    lifted = jnp.exp(scores - highest)
    weights = (lifted / lax.optimization_barrier(jnp.sum(lifted, axis=-1, keepdims=True))).astype(jnp.bfloat16)
    result = jnp.einsum('kgqn,nkd->qkgd', weights.astype(jnp.float32), value_part)
    return result.astype(jnp.bfloat16).reshape(row_count, kv_heads * group_size * HD)

def light_local(queries, keyed, valued, rates, doc_ids, prior_doc):
    running = jnp.cumsum(rates, axis=1)
    block_total = running[:, -1]
    places = jnp.arange(doc_ids.shape[0])
    spread = running[:, :, None] - running[:, None, :]
    visible = (places[None, :] <= places[:, None]) & (doc_ids[None, :] == doc_ids[:, None])
    decay_mask = jnp.where(visible[None], jnp.exp(jnp.minimum(spread, 0.0)), 0.0)
    scores = jnp.einsum('thd,shd->hts', queries.astype(jnp.float32), keyed.astype(jnp.float32))
    weights = (scores * decay_mask).astype(jnp.bfloat16)
    inside = jnp.einsum('hts,shd->thd', weights.astype(jnp.float32), valued.astype(jnp.float32))
    reach_factor = jnp.exp(running) * (doc_ids == prior_doc).astype(jnp.float32)[None, :]
    fading = jnp.exp(block_total[:, None] - running) * (doc_ids == doc_ids[-1]).astype(jnp.float32)[None, :]
    scaled = keyed.astype(jnp.float32) * jnp.transpose(fading)[:, :, None]
    added_state = jnp.einsum('shd,she->hde', scaled, valued.astype(jnp.float32), precision=lax.Precision.HIGHEST)
    carry_factor = jnp.exp(block_total) * (doc_ids[-1] == prior_doc).astype(jnp.float32)
    return (inside, reach_factor, added_state, carry_factor)

def reference(sparse_query, sparse_key, sparse_value, light_query, light_key, log_decay, segments, block_list):
    kv_all = jnp.concatenate([sparse_key, sparse_value], axis=1).reshape(QBLK, BLK, 2 * KVH * HD)
    seg_blocks = segments.reshape(QBLK, BLK)
    query_blocks = sparse_query.reshape(QBLK, BLK, ASKER_CHANNELS * HD)

    def one_block(block_item):
        query, own_kv, own_seg, listed = block_item
        safe_index = jnp.clip(listed, 0, QBLK - 1).astype(jnp.int32)
        return attend_block(query, own_kv, own_seg, kv_all[safe_index], seg_blocks[safe_index], listed >= 0)
    sparse_out = lax.map(one_block, (query_blocks, kv_all, seg_blocks, block_list)).reshape(SEQUENCE_LENGTH, ASKER_CHANNELS * HD)
    light_q = light_query.reshape(QBLK, BLK, ASKER_CHANNELS, HD)
    light_k = light_key.reshape(QBLK, BLK, ASKER_CHANNELS, HD)
    light_v = sparse_out.reshape(QBLK, BLK, ASKER_CHANNELS, HD)
    rate_blocks = jnp.transpose(log_decay.reshape(ASKER_CHANNELS, QBLK, BLK), (1, 0, 2))
    prior_docs = jnp.concatenate([jnp.full((1,), -1, jnp.int32), seg_blocks[:-1, -1].astype(jnp.int32)])

    def advance(carried, block_item):
        queries, keyed, valued, rates, doc_ids, prior_doc = block_item
        inside, reach_factor, added_state, carry_factor = light_local(queries, keyed, valued, rates, doc_ids, prior_doc)
        outside = jnp.einsum('thd,hde->the', queries.astype(jnp.float32), carried, precision=lax.Precision.HIGHEST) * jnp.transpose(reach_factor)[:, :, None]
        return (carry_factor[:, None, None] * carried + added_state, inside + outside)
    start_state = jnp.zeros((ASKER_CHANNELS, HD, HD), jnp.float32)
    final_state, lightning = lax.scan(advance, start_state, (light_q, light_k, light_v, rate_blocks, seg_blocks, prior_docs))
    lightning = lightning.reshape(SEQUENCE_LENGTH, ASKER_CHANNELS * HD)
    squares = lax.optimization_barrier(jnp.sum(lightning * lightning, axis=1))
    norm_scale = lax.rsqrt(squares / (ASKER_CHANNELS * HD) + norm_eps)
    return (sparse_out, (lightning * norm_scale[:, None]).astype(jnp.bfloat16))
```

```python
import functools

import jax
import jax.numpy as jnp
from jax import lax
from jax.experimental import pallas as pl
from jax.experimental.pallas import tpu as pltpu
from jax.sharding import PartitionSpec as P

ASKER_CHANNELS = 64
HD = 128
BLK = 128

NEG = -1e30
norm_eps = 1e-06
LOG2E = 1.4426950408889634
F32 = jnp.float32
BF16 = jnp.bfloat16


def nt(a, b):
    return lax.dot_general(a, b, (((1,), (1,)), ((), ())), preferred_element_type=F32)


def tn(a, b):
    return lax.dot_general(a, b, (((0,), (0,)), ((), ())), preferred_element_type=F32)


def nn(a, b):
    return lax.dot_general(a, b, (((1,), (0,)), ((), ())), preferred_element_type=F32)


def local_kernel(q_ref, k_ref, row_ref, col_ref, fade_ref, segc_ref, segr_ref, w_ref, kf_ref, bias):
    tokens = q_ref.shape[0]

    @pl.when(pl.program_id(0) == 0)
    def _():
        t = lax.broadcasted_iota(jnp.int32, (tokens, tokens), 0)
        s = lax.broadcasted_iota(jnp.int32, (tokens, tokens), 1)
        seen = (s <= t) & (segc_ref[...] == segr_ref[...])
        bias[...] = jnp.where(seen, 0.0, NEG)

    for i in range(w_ref.shape[0]):
        cols = slice(i * HD, (i + 1) * HD)
        k = k_ref[:, cols]
        spread = col_ref[0, :, i : i + 1] - row_ref[0, i : i + 1, :]
        w_ref[i] = (nt(q_ref[:, cols], k) * jnp.exp(spread + bias[...])).astype(BF16)
        kf_ref[:, cols] = (k.astype(F32) * fade_ref[0, :, i : i + 1]).astype(BF16)


def local_part(light_q, light_k, running, fading, segments, per_step):
    tokens, width = light_q.shape
    heads = width // HD
    steps = heads // per_step
    running_col = jnp.transpose(running.reshape(steps, per_step, tokens), (0, 2, 1))
    fading_col = jnp.transpose(fading.reshape(steps, per_step, tokens), (0, 2, 1))
    wide = pl.BlockSpec((tokens, per_step * HD), lambda g: (0, g))
    col = pl.BlockSpec((1, tokens, per_step), lambda g: (g, 0, 0))
    return pl.pallas_call(
        local_kernel,
        grid=(steps,),
        in_specs=[
            wide,
            wide,
            pl.BlockSpec((1, per_step, tokens), lambda g: (g, 0, 0)),
            col,
            col,
            pl.BlockSpec((tokens, 1), lambda g: (0, 0)),
            pl.BlockSpec((1, tokens), lambda g: (0, 0)),
        ],
        out_specs=[pl.BlockSpec((per_step, tokens, tokens), lambda g: (g, 0, 0)), wide],
        out_shape=[
            jax.ShapeDtypeStruct((heads, tokens, tokens), BF16),
            jax.ShapeDtypeStruct((tokens, width), BF16),
        ],
        scratch_shapes=[pltpu.VMEM((tokens, tokens), F32)],
        cost_estimate=pl.CostEstimate(
            flops=2 * heads * tokens * tokens * HD,
            bytes_accessed=3 * 2 * tokens * width + 2 * heads * tokens * tokens,
            transcendentals=heads * tokens * tokens,
        ),
        name="local_scores",
    )(
        light_q,
        light_k,
        running.reshape(steps, per_step, tokens),
        running_col,
        fading_col,
        segments[:, None],
        segments[None, :],
    )


def attend_kernel(group_sizes, table, *refs):
    pieces = len(group_sizes)
    q_ref, own_k, own_v, kf_ref, segc_ref, segr_ref = refs[:6]
    piece_k = refs[6 : 6 + pieces]
    piece_v = refs[6 + pieces : 6 + 2 * pieces]
    out_ref, state_ref, qs, scores, high, acc = refs[6 + 2 * pieces :]
    tokens, width = q_ref.shape
    blocks = tokens // BLK
    group = width // HD
    rows = group * BLK
    factor = HD ** (-0.5) * LOG2E
    ones = jnp.ones((BLK, HD), BF16)
    lane = lax.broadcasted_iota(jnp.int32, (BLK, BLK), 1)
    sub = lax.broadcasted_iota(jnp.int32, (BLK, BLK), 0)
    first_doc = table[0]

    def masked(score, ok):
        return jnp.where(ok[None], score.reshape(group, BLK, BLK), NEG).reshape(rows, BLK)

    for b in range(blocks):
        here = slice(b * BLK, (b + 1) * BLK)
        for h in range(group):
            qs[b, h * BLK : (h + 1) * BLK, :] = q_ref[here, h * HD : (h + 1) * HD]
        ok = (lane <= sub) & (segc_ref[here, :] == segr_ref[:, here])
        score = masked(nt(qs[b], own_k[here, :]), ok)
        scores[b] = score
        high[b] = score

    def each_piece(do):
        at = 0
        for i, size in enumerate(group_sizes):
            if size == 1:
                do(i, at, 0)
            else:

                def step(j, carry, i=i, at=at):
                    do(i, at + j, j)
                    return carry

                lax.fori_loop(0, size, step, 0)
            at += size

    def place(i, slot, j):
        base = 1 + 5 * slot
        start = pl.multiple_of(j * tokens + table[base + 2] * BLK, BLK)
        return table[base], table[base + 1], pl.ds(start, BLK), table[base + 3], table[base + 4]

    def first(i, slot, j):
        seen, b, span, least, to = place(i, slot, j)

        @pl.when(seen > 0)
        def _():
            here = pl.ds(pl.multiple_of(b * BLK, BLK), BLK)
            ok = (lane >= least) & (segc_ref[here, :] == first_doc)
            score = masked(nt(qs[b], piece_k[i][span, :]), ok)
            scores[blocks + to] = score
            high[b] = jnp.maximum(high[b], score)

    each_piece(first)

    for b in range(blocks):
        here = slice(b * BLK, (b + 1) * BLK)
        top = jnp.broadcast_to(jnp.max(high[b], axis=1, keepdims=True), (rows, BLK))
        high[b] = top
        weight = jnp.exp2((scores[b] - top) * factor).astype(BF16)
        acc[b] = nn(weight, jnp.concatenate([own_v[here, :], ones], axis=1))

    def second(i, slot, j):
        seen, b, span, least, to = place(i, slot, j)

        @pl.when(seen > 0)
        def _():
            weight = jnp.exp2((scores[blocks + to] - high[b]) * factor).astype(BF16)
            acc[b] += nn(weight, jnp.concatenate([piece_v[i][span, :], ones], axis=1))

    each_piece(second)

    for b in range(blocks):
        here = slice(b * BLK, (b + 1) * BLK)
        result = (acc[b, :, :HD] / acc[b, :, HD:]).astype(BF16)
        for h in range(group):
            out_ref[here, h * HD : (h + 1) * HD] = result[h * BLK : (h + 1) * BLK, :]
    for h in range(group):
        cols = slice(h * HD, (h + 1) * HD)
        state_ref[h] = tn(kf_ref[:, cols], out_ref[:, cols]).astype(BF16)


def attend_part(table, slots, query, own, faded, segments, pieces, chunk, chunks):
    tokens = query.shape[0]
    kv_here = own.shape[1] // (2 * HD)
    kv_heads = kv_here * chunks
    group = query.shape[1] // (kv_heads * HD)
    width = group * HD
    blocks = tokens // BLK
    sizes = tuple(p.shape[0] // tokens for p in pieces)
    first = chunk * kv_here

    def piece_specs(off):
        return [
            pl.BlockSpec((p.shape[0], HD), lambda g, table, off=off: (0, off + g)) for p in pieces
        ]

    def own_spec(off):
        return pl.BlockSpec((tokens, HD), lambda g, table: (0, off + g))

    wide = pl.BlockSpec((tokens, width), lambda g, table: (0, first + g))
    return pl.pallas_call(
        functools.partial(attend_kernel, sizes),
        grid_spec=pltpu.PrefetchScalarGridSpec(
            num_scalar_prefetch=1,
            grid=(kv_here,),
            in_specs=[
                wide,
                own_spec(0),
                own_spec(kv_here),
                wide,
                pl.BlockSpec((tokens, 1), lambda g, table: (0, 0)),
                pl.BlockSpec((1, tokens), lambda g, table: (0, 0)),
            ]
            + piece_specs(0)
            + piece_specs(kv_here),
            out_specs=[
                pl.BlockSpec((tokens, width), lambda g, table: (0, g)),
                pl.BlockSpec((group, HD, HD), lambda g, table: (g, 0, 0)),
            ],
            scratch_shapes=[
                pltpu.VMEM((blocks, group * BLK, HD), BF16),
                pltpu.VMEM((blocks + slots, group * BLK, BLK), F32),
                pltpu.VMEM((blocks, group * BLK, BLK), F32),
                pltpu.VMEM((blocks, group * BLK, 2 * HD), F32),
            ],
        ),
        out_shape=[
            jax.ShapeDtypeStruct((tokens, kv_here * width), BF16),
            jax.ShapeDtypeStruct((kv_here * group, HD, HD), BF16),
        ],
        compiler_params=pltpu.CompilerParams(vmem_limit_bytes=56 * 1024 * 1024),
        cost_estimate=pl.CostEstimate(
            flops=kv_here * group * 10 * 6 * BLK * BLK * HD,
            bytes_accessed=kv_here * (3 * 2 * tokens * width + 12 * 4 * tokens * HD),
            transcendentals=kv_here * group * 10 * BLK * BLK,
        ),
        name="attend",
    )(table, query, own, own, faded, segments[:, None], segments[None, :], *pieces, *pieces)


def output_kernel(w_ref, v_ref, q_ref, reach_ref, state_ref, out_ref, squares_ref):
    @pl.when(pl.program_id(0) == 0)
    def _():
        squares_ref[...] = jnp.zeros_like(squares_ref)

    total = squares_ref[...]
    for i in range(w_ref.shape[0]):
        cols = slice(i * HD, (i + 1) * HD)
        outside = nn(q_ref[:, cols], state_ref[i]) * reach_ref[0, :, i : i + 1]
        result = nn(w_ref[i], v_ref[:, cols]) + outside
        out_ref[:, cols] = result
        total += result * result
    squares_ref[...] = total


def output_part(weights, valued, light_q, reach, states, per_step, chunk, chunks):
    tokens, width = valued.shape
    heads = width // HD
    steps = heads // per_step
    first = chunk * steps
    all_steps = steps * chunks
    reach_col = jnp.transpose(reach.reshape(all_steps, per_step, tokens), (0, 2, 1))
    return pl.pallas_call(
        output_kernel,
        grid=(steps,),
        in_specs=[
            pl.BlockSpec((per_step, tokens, tokens), lambda g: (first + g, 0, 0)),
            pl.BlockSpec((tokens, per_step * HD), lambda g: (0, g)),
            pl.BlockSpec((tokens, per_step * HD), lambda g: (0, first + g)),
            pl.BlockSpec((1, tokens, per_step), lambda g: (first + g, 0, 0)),
            pl.BlockSpec((per_step, HD, HD), lambda g: (g, 0, 0)),
        ],
        out_specs=[
            pl.BlockSpec((tokens, per_step * HD), lambda g: (0, g)),
            pl.BlockSpec((tokens, HD), lambda g: (0, 0)),
        ],
        out_shape=[
            jax.ShapeDtypeStruct((tokens, width), F32),
            jax.ShapeDtypeStruct((tokens, HD), F32),
        ],
        cost_estimate=pl.CostEstimate(
            flops=heads * 2 * tokens * HD * (tokens + HD),
            bytes_accessed=heads * (2 * tokens * tokens + 8 * tokens * HD + 2 * HD * HD),
            transcendentals=0,
        ),
        name="outputs",
    )(weights, valued, light_q, reach_col, states)


def moved(value, pairs):
    return lax.ppermute(value, "seq", pairs)


def window_relay(own, shards):
    up = [(i, i + 4) for i in range(shards - 4)]
    cross = [(i, i ^ 2) for i in range(shards)]
    core = [(i, i ^ 1) for i in range(shards)]
    right = [(i, i ^ 2) for i in range(shards) if not i & 2]
    left = [(i, i ^ 2) for i in range(shards) if i & 2]
    below = moved(own, up)
    beside = moved(own, right)
    second = moved(below, up)
    below_beside = moved(below, cross)
    second_beside = moved(second, left)
    mine = [below, second, beside, below_beside, second_beside]
    return mine + [moved(part, core) for part in [own] + mine]


def window_owners(me):
    mine = jnp.stack([me - 4, me - 8, me ^ 2, (me ^ 2) - 4, (me ^ 2) - 8])
    usable = jnp.stack([me >= 0, me >= 0, (me & 2) > 0, me >= 0, (me & 2) == 0])
    far = jnp.stack([me ^ 1] + [(me ^ 1) - 4, (me ^ 1) - 8, me ^ 3, (me ^ 3) - 4, (me ^ 3) - 8])
    owners = jnp.concatenate([mine, far])
    usable = jnp.concatenate([usable, jnp.ones((1,), bool), usable])
    return jnp.where(usable, owners, -1)


def carried_in_planes(state, passing, me, shards):
    heads = state.shape[0]
    up = [(i, i + 4) for i in range(shards - 4)]
    cross = [(i, i ^ 2) for i in range(shards)]
    core = [(i, i ^ 1) for i in range(shards)]
    c, x = me & 1, (me >> 1) & 1
    halves = state.reshape(2, heads // 2, HD, HD)
    half_pass = passing.reshape(shards, 2, 2, heads // 4)[:, c]

    def pick(value, index):
        return lax.dynamic_index_in_dim(value, index, 0, keepdims=False)

    def times(factor, value):
        return factor[:, None, None] * value.astype(F32)

    def send(value, pairs):
        return moved(value.astype(BF16), pairs)

    plane = me & ~3
    near = pick(halves, c)
    far = send(pick(halves, 1 - c), core)
    core0 = jnp.where(c == 0, near, far)
    core1 = jnp.where(c == 0, far, near)

    def passed(position):
        return pick(half_pass, jnp.maximum(position, 0))

    flat = lambda p: p.reshape(heads // 2)
    chip = times(flat(passed((me & ~1) + 1)), core0) + core1.astype(F32)
    quarters = chip.reshape(2, heads // 4, HD, HD)
    near_q = pick(quarters, x)
    far_q = send(pick(quarters, 1 - x), cross).astype(F32)
    chip0 = jnp.where(x == 0, near_q, far_q)
    chip1 = jnp.where(x == 0, far_q, near_q)
    quarter = lambda p: pick(p, x)
    pass0 = quarter(passed(plane) * passed(plane + 1))
    pass1 = quarter(passed(plane + 2) * passed(plane + 3))
    plane_state = times(pass1, chip0) + chip1
    one_below = send(plane_state, up)
    two_below = send(one_below, up)
    lower = plane - 4
    pass_plane = quarter(passed(lower) * passed(lower + 1) * passed(lower + 2) * passed(lower + 3))
    entering0 = one_below.astype(F32) + times(pass_plane, two_below)
    entering1 = times(pass0, entering0) + chip0
    keep = jnp.where(x == 0, entering0, entering1).astype(BF16)
    got = send(jnp.where(x == 0, entering1, entering0), cross)
    both = jnp.where(
        x == 0, jnp.concatenate([keep, got], axis=0), jnp.concatenate([got, keep], axis=0)
    )
    after = times(flat(passed(me & ~1)), both) + core0.astype(F32)
    mine = jnp.where(c == 0, both, after.astype(BF16))
    other = send(jnp.where(c == 0, after, both.astype(F32)), core)
    return jnp.where(
        c == 0, jnp.concatenate([mine, other], axis=0), jnp.concatenate([other, mine], axis=0)
    )


def carried_in_any(state, passing, me, shards):
    states = lax.all_gather(state, "seq")
    place = jnp.arange(shards)

    def turn(j, total):
        part = passing[j][:, None, None] * total + states[j].astype(F32)
        return jnp.where(j < me, part, total)

    return lax.fori_loop(0, shards, turn, jnp.zeros(state.shape, F32)).astype(BF16)


def body(
    sparse_query, sparse_key, sparse_value, light_query, light_key, log_decay, segments, block_list
):
    tokens = sparse_query.shape[0]
    blocks = tokens // BLK
    kv_heads = sparse_key.shape[1] // HD
    heads = light_query.shape[1] // HD
    group = heads // kv_heads
    shards = lax.axis_size("seq")
    me = lax.axis_index("seq")
    planes = shards == 16
    chunks = 2 if kv_heads % 2 == 0 and planes else 1
    kv_chunk = kv_heads // chunks * HD
    head_chunk = heads // chunks

    owns = []
    pieces = []
    for chunk in range(chunks):
        cols = slice(chunk * kv_chunk, (chunk + 1) * kv_chunk)
        own = jnp.concatenate([sparse_key[:, cols], sparse_value[:, cols]], axis=1)
        owns.append(own)
        if planes:
            pieces.append(window_relay(own, shards))
        else:
            pieces.append([lax.all_gather(own, "seq", axis=0, tiled=True)])
    owners = window_owners(me) if planes else jnp.where(jnp.arange(shards) < me, jnp.arange(shards), -1)

    upper = (jnp.arange(tokens)[:, None] <= jnp.arange(tokens)[None, :]).astype(F32)
    running = jnp.dot(log_decay, upper, precision=lax.Precision.HIGHEST)
    totals = running[:, -1]
    counts = jnp.sum(segments[None, :] < jnp.arange(1, 4)[:, None], axis=1)
    info = jnp.concatenate(
        [totals, counts.astype(F32), segments[:1].astype(F32), segments[-1:].astype(F32)]
    )
    info = jnp.pad(info, (0, 128 - info.shape[0]))
    known = lax.all_to_all(jnp.broadcast_to(info, (shards, 128)), "seq", 0, 0, tiled=True)
    starts = jnp.concatenate([jnp.zeros((1,), F32), jnp.sum(known[:, heads : heads + 3], axis=0)])
    firsts, lasts = known[:, heads + 3], known[:, heads + 4]
    begins = jnp.sum(
        jnp.where(firsts[:, None] == jnp.arange(4)[None, :], starts[None, :], 0.0), axis=1
    )
    begun = begins < (jnp.arange(shards) * tokens).astype(F32)
    passing = jnp.exp(known[:, :heads]) * (begun & (firsts == lasts)).astype(F32)[:, None]

    first_doc, last_doc = segments[0], segments[-1]
    doc_begin = jnp.sum(jnp.where(jnp.arange(4) == first_doc, starts, 0.0)).astype(jnp.int32)
    carried_on = doc_begin < me * tokens
    fading = jnp.exp(totals[:, None] - running) * (segments == last_doc).astype(F32)[None, :]
    reach = jnp.exp(running) * ((segments == first_doc) & carried_on).astype(F32)[None, :]

    named = (block_list[None] >= 0) & (block_list[None] // blocks == owners[:, None, None])
    hit = jnp.sum(jnp.where(named, block_list[None] + 1, 0), axis=2)
    asker = jnp.sum(jnp.where(hit > 0, jnp.arange(blocks)[None, :], 0), axis=1)
    listed = jnp.sum(hit, axis=1) - 1
    least = doc_begin - listed * BLK
    seen = (listed >= 0) & (least < BLK)
    slots = min(owners.shape[0], blocks * block_list.shape[1])
    order = jnp.minimum(jnp.cumsum(seen.astype(jnp.int32)) - 1, slots - 1)
    order = jnp.maximum(order, 0)
    rows = jnp.stack(
        [seen.astype(jnp.int32), asker, jnp.maximum(listed, 0) % blocks, least, order], axis=1
    )
    table = jnp.concatenate([first_doc[None], rows.reshape(-1)]).astype(jnp.int32)

    weights, faded = local_part(light_query, light_key, running, fading, segments, group)

    outs, results, squares = [], [], 0.0
    for chunk in range(chunks):
        attended, state = attend_part(
            table, slots, sparse_query, owns[chunk], faded, segments, pieces[chunk], chunk, chunks
        )
        outs.append(attended)
        span = slice(chunk * head_chunk, (chunk + 1) * head_chunk)
        carry = carried_in_planes if planes else carried_in_any
        entering = carry(state, passing[:, span], me, shards)
        result, square = output_part(
            weights, attended, light_query, reach, entering, group, chunk, chunks
        )
        results.append(result)
        squares = squares + jnp.sum(square, axis=1)
    squares = lax.psum(squares, "head")
    scale = lax.rsqrt(squares / (ASKER_CHANNELS * HD) + norm_eps)
    mixed = jnp.concatenate([(r * scale[:, None]).astype(BF16) for r in results], axis=1)
    return (jnp.concatenate(outs, axis=1), mixed)


def solution(mesh):
    in_specs = (
        P("seq", "head"),
        P("seq", "head"),
        P("seq", "head"),
        P("seq", "head"),
        P("seq", "head"),
        P("head", "seq"),
        P("seq"),
        P("seq", None),
    )
    out_specs = (P("seq", "head"), P("seq", "head"))
    return jax.shard_map(body, mesh=mesh, in_specs=in_specs, out_specs=out_specs, check_vma=False)
```

```python
import functools

import jax
import jax.numpy as jnp
from jax import lax
from jax.experimental import pallas as pl
from jax.experimental.pallas import tpu as pltpu
from jax.sharding import PartitionSpec as P

ASKER_CHANNELS = 64
HD = 128
BLK = 128

NEG = -1e30
norm_eps = 1e-06
LOG2E = 1.4426950408889634
F32 = jnp.float32
BF16 = jnp.bfloat16
CLASSES = (1, 2, 3, 5, 7, 9)


def room(mib):
    return pltpu.CompilerParams(vmem_limit_bytes=mib * 1024 * 1024)


def far(value):
    return pltpu.with_memory_space_constraint(value, pltpu.HBM)


def nt(a, b):
    return lax.dot_general(a, b, (((1,), (1,)), ((), ())), preferred_element_type=F32)


def tn(a, b):
    return lax.dot_general(a, b, (((0,), (0,)), ((), ())), preferred_element_type=F32)


def nn(a, b):
    return lax.dot_general(a, b, (((1,), (0,)), ((), ())), preferred_element_type=F32)


def info_kernel(decay_ref, seg_ref, info_ref):
    rows, lanes = info_ref.shape
    heads, tokens = decay_ref.shape
    ones = jnp.ones((rows, tokens), F32)
    totals = lax.dot_general(
        ones,
        decay_ref[...],
        (((1,), (1,)), ((), ())),
        precision=lax.Precision.HIGHEST,
        preferred_element_type=F32,
    )
    info_ref[...] = jnp.zeros((rows, lanes), F32)
    info_ref[:, :heads] = totals
    seg = seg_ref[...]
    for doc in range(1, 4):
        count = jnp.sum((seg < doc).astype(F32), axis=1, keepdims=True)
        info_ref[:, heads + doc - 1 : heads + doc] = jnp.broadcast_to(count, (rows, 1))
    ends = seg.astype(F32)
    info_ref[:, heads + 3 : heads + 4] = jnp.broadcast_to(ends[:, :1], (rows, 1))
    info_ref[:, heads + 4 : heads + 5] = jnp.broadcast_to(ends[:, tokens - 1 :], (rows, 1))


def own_info(log_decay, seg_row, shards):
    return pl.pallas_call(
        info_kernel,
        out_shape=jax.ShapeDtypeStruct((shards, 128), F32),
        compiler_params=room(2),
        name="own_info",
    )(log_decay, seg_row)


def passing_kernel(heads, tokens, known_ref, passing_ref):
    known = known_ref[...]
    rows = known.shape[0]
    firsts, lasts = known[:, heads + 3 : heads + 4], known[:, heads + 4 : heads + 5]
    begins = jnp.zeros_like(firsts)
    for doc in range(1, 4):
        start = jnp.sum(known[:, heads + doc - 1 : heads + doc], axis=0, keepdims=True)
        begins = jnp.where(firsts == doc, start, begins)
    position = lax.broadcasted_iota(jnp.int32, (rows, 1), 0) * tokens
    begun = begins < position.astype(F32)
    through = begun & (firsts == lasts)
    lane = lax.broadcasted_iota(jnp.int32, known.shape, 1)
    decay = jnp.exp(jnp.where(lane < heads, known, 0.0))
    passing_ref[...] = jnp.where(lane == heads, begun.astype(F32), jnp.where(through, decay, 0.0))


def all_passing(known, heads, tokens):
    return pl.pallas_call(
        functools.partial(passing_kernel, heads, tokens),
        out_shape=jax.ShapeDtypeStruct(known.shape, F32),
        compiler_params=room(2),
        name="passing",
    )(known)


def local_kernel(q_ref, k_ref, decay_ref, segc_ref, segr_ref, w_ref, kf_ref, qf_ref, bias, upper):
    tokens = q_ref.shape[0]

    @pl.when(pl.program_id(0) == 0)
    def _():
        t = lax.broadcasted_iota(jnp.int32, (tokens, tokens), 0)
        s = lax.broadcasted_iota(jnp.int32, (tokens, tokens), 1)
        seen = (s <= t) & (segc_ref[...] == segr_ref[...])
        bias[...] = jnp.where(seen, 0.0, NEG)
        upper[...] = (t <= s).astype(F32)

    row = lax.dot_general(
        decay_ref[...],
        upper[...],
        (((1,), (0,)), ((), ())),
        precision=lax.Precision.HIGHEST,
        preferred_element_type=F32,
    )
    seg = segc_ref[...]
    col = jnp.transpose(row)
    fade = jnp.where(seg == seg[tokens - 1 :, :], jnp.exp(col[tokens - 1 :, :] - col), 0.0)
    reach = jnp.where(seg == seg[:1, :], jnp.exp(col), 0.0)
    for i in range(w_ref.shape[0]):
        cols = slice(i * HD, (i + 1) * HD)
        k = k_ref[:, cols]
        q = q_ref[:, cols]
        spread = col[:, i : i + 1] - row[i : i + 1, :]
        w_ref[i] = (nt(q, k) * jnp.exp(spread + bias[...])).astype(BF16)
        kf_ref[i] = jnp.transpose((k.astype(F32) * fade[:, i : i + 1]).astype(BF16))
        qf_ref[:, cols] = (q.astype(F32) * reach[:, i : i + 1]).astype(BF16)


def local_part(light_q, light_k, log_decay, seg_col, seg_row, per_step):
    tokens, width = light_q.shape
    heads = width // HD
    steps = heads // per_step
    wide = pl.BlockSpec((tokens, per_step * HD), lambda g: (0, g))
    return pl.pallas_call(
        local_kernel,
        grid=(steps,),
        in_specs=[
            wide,
            wide,
            pl.BlockSpec((per_step, tokens), lambda g: (g, 0)),
            pl.BlockSpec((tokens, 1), lambda g: (0, 0)),
            pl.BlockSpec((1, tokens), lambda g: (0, 0)),
        ],
        out_specs=[
            pl.BlockSpec((per_step, tokens, tokens), lambda g: (g, 0, 0)),
            pl.BlockSpec((per_step, HD, tokens), lambda g: (g, 0, 0)),
            wide,
        ],
        out_shape=[
            jax.ShapeDtypeStruct((heads, tokens, tokens), BF16),
            jax.ShapeDtypeStruct((heads, HD, tokens), BF16),
            jax.ShapeDtypeStruct((tokens, width), BF16),
        ],
        scratch_shapes=[pltpu.VMEM((tokens, tokens), F32), pltpu.VMEM((tokens, tokens), F32)],
        compiler_params=room(14),
        cost_estimate=pl.CostEstimate(
            flops=2 * heads * tokens * tokens * HD,
            bytes_accessed=4 * 2 * tokens * width + 2 * heads * tokens * tokens,
            transcendentals=heads * tokens * tokens,
        ),
        name="local_scores",
    )(far(light_q), far(light_k), log_decay, seg_col, seg_row)


def table_kernel(sizes, planes, heads, listing, known, place_ref, segc_ref, segr_ref, *refs):
    own_bias, row_bias, key_bias, table, named, counts = refs
    tokens = segc_ref.shape[0]
    blocks = tokens // BLK
    shards = known.shape[0]
    per_row = listing.shape[0] // blocks
    total = sum(sizes)
    me = place_ref[0]
    first_doc = known[me, heads + 3].astype(jnp.int32)
    begin = known[0, heads] * 0.0
    for doc in range(1, 4):
        start = known[0, heads + doc - 1]
        for j in range(1, shards):
            start = start + known[j, heads + doc - 1]
        begin = jnp.where(first_doc == doc, start, begin)
    begin = begin.astype(jnp.int32)
    for delta in range(shards):
        named[delta] = 0
    for b in range(blocks):
        counts[b] = 0
    for e in range(listing.shape[0]):
        entry = listing[e]
        delta = jnp.where(entry >= 0, me - lax.div(jnp.maximum(entry, 0), blocks), 0)
        named[delta] = 1 + (e // per_row) * blocks + lax.rem(jnp.maximum(entry, 0), blocks)
    named[0] = 0
    key_bias[...] = jnp.full(key_bias.shape, NEG, F32)
    lane = lax.broadcasted_iota(jnp.int32, (BLK, BLK), 1)
    sub = lax.broadcasted_iota(jnp.int32, (BLK, BLK), 0)
    for b in range(blocks):
        here = slice(b * BLK, (b + 1) * BLK)
        ok = (lane <= sub) & (segc_ref[here, :] == segr_ref[:, here])
        own_bias[b] = jnp.where(ok, 0.0, NEG)
        ok = jnp.broadcast_to(segc_ref[here, :], (BLK, BLK)) == first_doc
        row_bias[b] = jnp.where(ok, 0.0, NEG)

    def fill(slot, owner, usable):
        usable = usable & (owner >= 0) & (owner < me)
        code = named[jnp.where(usable, me - owner, 0)] - 1
        half = lax.rem(jnp.maximum(code, 0), blocks)
        least = begin - (owner * blocks + half) * BLK
        seen = usable & (code >= 0) & (least < BLK)
        b = lax.div(jnp.maximum(code, 0), blocks)
        to = jnp.where(seen, counts[b] + 1, 0)
        table[3 * slot] = b * (1 + per_row) + to
        table[3 * slot + 1] = half
        table[3 * slot + 2] = seen.astype(jnp.int32)

        @pl.when(seen)
        def _():
            counts[b] = to
            at = b * (1 + per_row) + to
            key_bias[pl.ds(at, 1)] = jnp.where(lane[:8] >= least, 0.0, NEG)[None]

    if planes:
        for slot, (owner, usable) in enumerate(window_owners(me)):
            fill(slot, owner, usable)
    else:

        def fill_step(j, carry):
            fill(j, j, j >= 0)
            return carry

        lax.fori_loop(0, shards, fill_step, 0)
    for b in range(blocks):
        table[3 * total + b] = counts[b]


def seen_table(place, listing, known, seg_col, seg_row, sizes, heads, planes):
    blocks = seg_col.shape[0] // BLK
    tiles = listing.shape[0] + blocks
    smem = pl.BlockSpec(memory_space=pltpu.SMEM)
    vmem = pl.BlockSpec(memory_space=pltpu.VMEM)
    return pl.pallas_call(
        functools.partial(table_kernel, sizes, planes, heads),
        in_specs=[smem, smem, smem, vmem, vmem],
        out_specs=[vmem, vmem, vmem, smem],
        out_shape=[
            jax.ShapeDtypeStruct((blocks, BLK, BLK), F32),
            jax.ShapeDtypeStruct((blocks, BLK, BLK), F32),
            jax.ShapeDtypeStruct((tiles, 8, BLK), F32),
            jax.ShapeDtypeStruct((3 * sum(sizes) + blocks,), jnp.int32),
        ],
        scratch_shapes=[
            pltpu.SMEM((known.shape[0],), jnp.int32),
            pltpu.SMEM((blocks,), jnp.int32),
        ],
        compiler_params=room(6),
        name="seen_table",
    )(listing, known, place, seg_col, seg_row)


def attend_kernel(sizes, kv_step, kv_head, table, *refs):
    pieces = len(sizes)
    q_ref, own_k, own_v, kf_ref, own_bias, row_bias, key_bias = refs[:7]
    piece = refs[7 : 7 + pieces]
    out_ref, state_ref, keys, values, sems = refs[-5:]
    tokens, width = q_ref.shape
    blocks = tokens // BLK
    group = width // HD
    per_row = keys.shape[0] // (blocks * BLK) - 1
    factor = HD ** (-0.5) * LOG2E
    total = sum(sizes)

    def each_piece(do):
        at = 0
        for i, size in enumerate(sizes):
            if size == 1:
                do(i, at, 0)
            else:

                def step(j, carry, i=i, at=at):
                    do(i, at + j, j)
                    return carry

                lax.fori_loop(0, size, step, 0)
            at += size

    def copies(i, slot, j):
        span = pl.ds(pl.multiple_of(j * tokens + table[3 * slot + 1] * BLK, BLK), BLK)
        to = pl.ds(pl.multiple_of(table[3 * slot] * BLK, BLK), BLK)
        for part, buffer in enumerate((keys, values)):
            cols = pl.ds(pl.multiple_of((kv_head[1] + part * kv_step) * HD, HD), HD)
            yield pltpu.make_async_copy(piece[i].at[span, cols], buffer.at[to, :], sems.at[part, slot])

    def bring(i, slot, j):
        @pl.when(table[3 * slot + 2] > 0)
        def _():
            for copy in copies(i, slot, j):
                copy.start()

    def arrive(i, slot, j):
        @pl.when(table[3 * slot + 2] > 0)
        def _():
            for copy in copies(i, slot, j):
                copy.wait()

    each_piece(bring)
    for b in range(blocks):
        base = b * (1 + per_row) * BLK
        keys[base : base + BLK, :] = own_k[b * BLK : (b + 1) * BLK, :]
        values[base : base + BLK, :] = own_v[b * BLK : (b + 1) * BLK, :]
    each_piece(arrive)

    def heads_out(b, tiles, h, count):
        base = b * (1 + per_row)
        here = pl.ds(pl.multiple_of(b * BLK, BLK), BLK)
        span = pl.ds(pl.multiple_of(base * BLK, BLK), tiles * BLK)
        cols = [pl.ds(pl.multiple_of((h + j) * HD, HD), HD) for j in range(count)]
        query = jnp.concatenate([q_ref[here, c] for c in cols], axis=0)
        score = nt(query, keys[span, :]).reshape(count, BLK, tiles * BLK)
        bias = [own_bias[b]] + [row_bias[b] + key_bias[base + t][:1, :] for t in range(1, tiles)]
        score = score + jnp.concatenate(bias, axis=1)[None]
        lifted = jnp.exp2((score - jnp.max(score, axis=2, keepdims=True)) * factor)
        weight = lifted * (1.0 / jnp.sum(lifted, axis=2, keepdims=True))
        weight = weight.astype(BF16).reshape(count * BLK, tiles * BLK)
        result = nn(weight, values[span, :]).astype(BF16)
        for j, c in enumerate(cols):
            out_ref[here, c] = result[j * BLK : (j + 1) * BLK, :]

    classes = sorted({min(t, 1 + per_row) for t in CLASSES} | {1 + per_row})

    def block_out(b, carry):
        need = table[3 * total + b] + 1
        low = 0
        for tiles in classes:
            together = min(group, 8 if tiles <= 2 else 4 if tiles <= 5 else 2)

            @pl.when((need > low) & (need <= tiles))
            def _(low=low, tiles=tiles, together=together):
                for t in range(max(low + 1, 1), tiles):

                    @pl.when(t >= need)
                    def _(t=t):
                        start = pl.multiple_of((b * (1 + per_row) + t) * BLK, BLK)
                        keys[pl.ds(start, BLK), :] = jnp.zeros((BLK, HD), BF16)
                        values[pl.ds(start, BLK), :] = jnp.zeros((BLK, HD), BF16)

                def step(i, carry):
                    heads_out(b, tiles, i * together, together)
                    return carry

                lax.fori_loop(0, group // together, step, 0)

            low = tiles
        return carry

    lax.fori_loop(0, blocks, block_out, 0)
    for h in range(group):
        state_ref[h] = nn(kf_ref[h], out_ref[:, h * HD : (h + 1) * HD])


def attend_part(kv_head, table, biases, query, own, faded, pieces, sizes, kv_step, before):
    tokens = query.shape[0]
    group = faded.shape[0] * HD // own.shape[1] * 2
    width = group * HD
    wide = pl.BlockSpec((tokens, width), lambda g, *s: (0, s[0][0]))
    in_specs = [
        wide,
        pl.BlockSpec((tokens, HD), lambda g, *s: (0, s[0][1])),
        pl.BlockSpec((tokens, HD), lambda g, *s: (0, s[0][1] + kv_step)),
        pl.BlockSpec((group, HD, tokens), lambda g, *s: (s[0][0], 0, 0)),
    ]
    in_specs += [pl.BlockSpec(bias.shape, lambda g, *s: (0, 0, 0)) for bias in biases]
    in_specs += [pl.BlockSpec(memory_space=pl.ANY)] * len(pieces)
    operands = [far(query), own, own, faded, *biases, *pieces]
    aliases = {}
    if before is not None:
        aliases = {2 + len(operands): 0}
        in_specs.append(pl.BlockSpec(memory_space=pl.ANY))
        operands.append(before)
    rows = biases[2].shape[0] * BLK
    return pl.pallas_call(
        functools.partial(attend_kernel, sizes, kv_step),
        grid_spec=pltpu.PrefetchScalarGridSpec(
            num_scalar_prefetch=2,
            grid=(1,),
            in_specs=in_specs,
            out_specs=[wide, pl.BlockSpec((group, HD, HD), lambda g, *s: (0, 0, 0))],
            scratch_shapes=[
                pltpu.VMEM((rows, HD), BF16),
                pltpu.VMEM((rows, HD), BF16),
                pltpu.SemaphoreType.DMA((2, sum(sizes))),
            ],
        ),
        out_shape=[
            jax.ShapeDtypeStruct(query.shape, BF16),
            jax.ShapeDtypeStruct((group, HD, HD), F32),
        ],
        input_output_aliases=aliases,
        compiler_params=room(20),
        cost_estimate=pl.CostEstimate(
            flops=group * 10 * 6 * BLK * BLK * HD,
            bytes_accessed=3 * 2 * tokens * width + 12 * 4 * tokens * HD,
            transcendentals=group * 10 * BLK * BLK,
        ),
        name="attend",
    )(kv_head, table, *operands)


def inside_kernel(w_ref, v_ref, out_ref):
    for i in range(w_ref.shape[0]):
        cols = slice(i * HD, (i + 1) * HD)
        out_ref[:, cols] = nn(w_ref[i], v_ref[:, cols])


def inside_part(weights, valued, group):
    tokens, width = valued.shape
    steps = width // HD // group
    return pl.pallas_call(
        inside_kernel,
        grid=(steps,),
        in_specs=[
            pl.BlockSpec((group, tokens, tokens), lambda g: (g, 0, 0)),
            pl.BlockSpec((tokens, group * HD), lambda g: (0, g)),
        ],
        out_specs=pl.BlockSpec((tokens, group * HD), lambda g: (0, g)),
        out_shape=jax.ShapeDtypeStruct((tokens, width), F32),
        compiler_params=room(12),
        cost_estimate=pl.CostEstimate(
            flops=steps * group * 2 * tokens * tokens * HD,
            bytes_accessed=steps * group * (2 * tokens * tokens + 6 * tokens * HD),
            transcendentals=0,
        ),
        name="inside",
    )(weights, valued)


def output_kernel(planes, chunks, place_ref, q_ref, inside_ref, *refs):
    keeps, gots = refs[:chunks], refs[chunks : 2 * chunks]
    out_ref, squares_ref, total_ref = refs[-3:]
    step_at = pl.program_id(0)
    group = gots[0].shape[0]
    steps = pl.num_programs(0) // chunks

    @pl.when(step_at == 0)
    def _():
        total_ref[...] = jnp.zeros_like(total_ref)

    def part(state_of):
        total = total_ref[...]
        for i in range(group):
            cols = slice(i * HD, (i + 1) * HD)
            result = inside_ref[:, cols] + nn(q_ref[:, cols], state_of(i))
            out_ref[:, cols] = result
            total += result * result
        total_ref[...] = total

    for chunk in range(chunks):

        @pl.when((step_at >= chunk * steps) & (step_at < (chunk + 1) * steps))
        def _(chunk=chunk):
            keep_ref, got_ref = keeps[chunk], gots[chunk]
            if planes:
                mine = step_at - chunk * steps == (place_ref[0] & 1)
                part(lambda i: jnp.where(mine, keep_ref[i], got_ref[i]))
            else:
                part(lambda i: keep_ref[i])

    @pl.when(step_at == pl.num_programs(0) - 1)
    def _():
        squares_ref[...] = jnp.sum(jnp.transpose(total_ref[...]), axis=0, keepdims=True)


def output_part(place, inside, faded_q, states, group, planes):
    tokens, width = faded_q.shape
    chunks = len(states)
    steps = width // HD // group
    wide = pl.BlockSpec((tokens, group * HD), lambda g, *s: (0, g))
    keep = pl.BlockSpec((group, HD, HD), lambda g, *s: (0 if planes else g, 0, 0))
    got = pl.BlockSpec((group, HD, HD), lambda g, *s: (0, 0, 0))
    return pl.pallas_call(
        functools.partial(output_kernel, planes, chunks),
        grid_spec=pltpu.PrefetchScalarGridSpec(
            num_scalar_prefetch=1,
            grid=(steps,),
            in_specs=[wide, wide] + [keep] * chunks + [got] * chunks,
            out_specs=[wide, pl.BlockSpec((1, tokens), lambda g, *s: (0, 0))],
            scratch_shapes=[pltpu.VMEM((tokens, HD), F32)],
        ),
        out_shape=[
            jax.ShapeDtypeStruct((tokens, width), F32),
            jax.ShapeDtypeStruct((1, tokens), F32),
        ],
        compiler_params=room(16),
        cost_estimate=pl.CostEstimate(
            flops=2 * tokens * width * HD,
            bytes_accessed=10 * tokens * width + 2 * width * HD,
            transcendentals=0,
        ),
        name="outputs",
    )(place, faded_q, inside, *[k for k, _ in states], *[g for _, g in states])


def scale_kernel(features, squares_ref, value_ref, out_ref):
    tokens = value_ref.shape[0]
    row = lax.rsqrt(squares_ref[...] / features + norm_eps)
    scale = jnp.transpose(jnp.broadcast_to(row, (HD, tokens)))
    for i in range(value_ref.shape[1] // HD):
        cols = slice(i * HD, (i + 1) * HD)
        out_ref[:, cols] = (value_ref[:, cols] * scale).astype(BF16)


def scale_part(squares, value, per_step):
    tokens, width = value.shape
    wide = pl.BlockSpec((tokens, per_step * HD), lambda g: (0, g))
    return pl.pallas_call(
        functools.partial(scale_kernel, ASKER_CHANNELS * HD),
        grid=(width // HD // per_step,),
        in_specs=[pl.BlockSpec((1, tokens), lambda g: (0, 0)), wide],
        out_specs=wide,
        out_shape=jax.ShapeDtypeStruct((tokens, width), BF16),
        compiler_params=room(8),
        name="scaled",
    )(squares, value)


def moved(value, pairs):
    return lax.ppermute(value, "seq", pairs)


def up(shards):
    return [(i, (i + 4) % shards) for i in range(shards)]


def cross(shards):
    return [(i, i ^ 2) for i in range(shards)]


def core(shards):
    return [(i, i ^ 1) for i in range(shards)]


def after(values, *first):
    return lax.optimization_barrier((values, first))[0]


def window_owners(me):
    always = me >= 0
    right, left = (me & 2) > 0, (me & 2) == 0

    def seen_from(at):
        side = at ^ 2
        return [
            (at - 4, always),
            (at - 8, always),
            (side, right),
            (side - 4, always),
            (side - 8, left),
        ]

    return seen_from(me) + [(me ^ 1, always)] + seen_from(me ^ 1)


def mixing_kernel(body, passing, place_ref, *refs):
    me = place_ref[0]
    body(passing, me, me & 1, (me >> 1) & 1, *refs)


def mixing(name, body, passing, place, values, outs):
    smem = pl.BlockSpec(memory_space=pltpu.SMEM)
    vmem = pl.BlockSpec(memory_space=pltpu.VMEM)
    return pl.pallas_call(
        functools.partial(mixing_kernel, body),
        in_specs=[smem, smem] + [vmem] * len(values),
        out_specs=[vmem] * len(outs),
        out_shape=[jax.ShapeDtypeStruct((n, HD, HD), dtype) for n, dtype in outs],
        cost_estimate=pl.CostEstimate(
            flops=4 * sum(n for n, _ in outs) * HD * HD,
            bytes_accessed=8 * sum(n for n, _ in outs) * HD * HD,
            transcendentals=0,
        ),
        compiler_params=room(4),
        name=name,
    )(passing, place, *values)


def carried_in_planes(keep, send, passing, place, shards, head0, heads):
    half = keep.shape[0]
    quarter = half // 2
    def chip_body(passing, me, c, x, keep_ref, far_ref, near_ref, send_ref):
        base = head0 + c * half
        for part, to in ((x, near_ref), (1 - x, send_ref)):
            for i in range(quarter):
                h = part * quarter + i
                fade = passing[me | 1, base + h]
                a, b = jnp.where(c == 0, fade, 1.0), jnp.where(c == 0, 1.0, fade)
                to[i] = (keep_ref[h] * a + far_ref[h] * b).astype(to.dtype)

    def plane_body(passing, me, c, x, near_ref, far_ref, out_ref):
        base = head0 + c * half + x * quarter
        for i in range(quarter):
            fade = passing[me | 3, base + i] * passing[(me | 3) - 1, base + i]
            a, b = jnp.where(x == 0, fade, 1.0), jnp.where(x == 0, 1.0, fade)
            out_ref[i] = (near_ref[i] * a + far_ref[i].astype(F32) * b).astype(BF16)

    def enter_body(passing, me, c, x, near_ref, far_ref, one_ref, two_ref, keep_ref, send_ref):
        base = head0 + c * half + x * quarter
        plane = me & ~3
        low = jnp.maximum(plane - 4, 0)
        for i in range(quarter):
            h = base + i
            fade = passing[low, h] * passing[low + 1, h] * passing[low + 2, h] * passing[low + 3, h]
            e0 = jnp.where(me >= 4, one_ref[i].astype(F32), 0.0)
            e0 = jnp.where(me >= 8, e0 + two_ref[i].astype(F32) * fade, e0)
            chip = jnp.where(x == 0, near_ref[i], far_ref[i].astype(F32))
            e1 = e0 * (passing[plane, h] * passing[plane + 1, h]) + chip
            keep_ref[i] = jnp.where(x == 0, e0, e1)
            send_ref[i] = jnp.where(x == 0, e1, e0).astype(BF16)

    def core_body(passing, me, c, x, keep_ref, far_ref, near_ref, got_ref, mine_ref, send_ref):
        base = head0 + c * half
        mine_on, other_on = passing[me, heads], passing[me ^ 1, heads]
        for part, source in ((x, near_ref), (1 - x, got_ref)):
            for i in range(quarter):
                h = part * quarter + i
                e0 = source[i].astype(F32)
                first = jnp.where(c == 0, keep_ref[h], far_ref[h])
                e1 = e0 * passing[me & ~1, base + h] + first
                mine_ref[h] = (jnp.where(c == 0, e0, e1) * mine_on).astype(BF16)
                send_ref[h] = (jnp.where(c == 0, e1, e0) * other_on).astype(BF16)

    sent = moved(send, core(shards))
    near_q, send_q = mixing(
        "mix_chip", chip_body, passing, place, [keep, sent], [(quarter, F32), (quarter, BF16)]
    )
    far_q = moved(send_q, cross(shards))
    yield send_q
    (plane_state,) = mixing(
        "mix_plane", plane_body, passing, place, [near_q, far_q], [(quarter, BF16)]
    )
    one_below = moved(plane_state, up(shards))
    wait = yield plane_state
    if wait is not None:
        near_q = after(near_q, wait)
    two_below = moved(one_below, up(shards))
    near_e, send_e = mixing(
        "mix_enter",
        enter_body,
        passing,
        place,
        [near_q, far_q, one_below, two_below],
        [(quarter, F32), (quarter, BF16)],
    )
    got_e = moved(send_e, cross(shards))
    mine, other = mixing(
        "mix_core", core_body, passing, place, [keep, sent, near_e, got_e], [(half, BF16), (half, BF16)]
    )
    yield mine, moved(other, core(shards))


def carried_in_any(state, passing, me, shards):
    states = lax.all_gather(state, "seq")

    def turn(j, total):
        part = passing[j][:, None, None] * total + states[j].astype(F32)
        return jnp.where(j < me, part, total)

    return lax.fori_loop(0, shards, turn, jnp.zeros(state.shape, F32)).astype(BF16)


def body(
    sparse_query, sparse_key, sparse_value, light_query, light_key, log_decay, segments, block_list
):
    tokens = sparse_query.shape[0]
    kv_heads = sparse_key.shape[1] // HD
    heads = light_query.shape[1] // HD
    group = heads // kv_heads
    shards = lax.axis_size("seq")
    me = lax.axis_index("seq")
    place = me.astype(jnp.int32).reshape(1)
    planes = shards == 16 and kv_heads == 4
    chunks = 2 if planes else 1
    kv_chunk = kv_heads // chunks
    head_chunk = heads // chunks
    parts = []
    for chunk in range(chunks):
        cols = slice(chunk * kv_chunk * HD, (chunk + 1) * kv_chunk * HD)
        parts += [sparse_key[:, cols], sparse_value[:, cols]]
    own = jnp.concatenate(parts, axis=1)
    seg_col, seg_row, listing = segments[:, None], segments[None, :], block_list.reshape(-1)
    if planes:
        below, beside = moved(own, up(shards)), moved(own, cross(shards))
    else:
        pieces = [lax.all_gather(own, "seq", axis=0, tiled=True)]
    whiches = []
    for chunk in range(chunks):
        order = [1 - (me & 1), me & 1] if planes else range(kv_chunk)
        for kv_head in order:
            kv_head = jnp.asarray(kv_head, jnp.int32)
            at = [chunk * kv_chunk + kv_head, chunk * 2 * kv_chunk + kv_head]
            whiches.append(jnp.stack(at))
    info = own_info(log_decay, seg_row, shards)
    info, whiches, place, listing, seg_col = after((info, whiches, place, listing, seg_col), own)
    known = lax.all_to_all(info, "seq", 0, 0, tiled=True)
    passing = all_passing(known, heads, tokens)
    sizes = (1,) * 11 if planes else (shards,)
    *biases, table = seen_table(place, listing, known, seg_col, seg_row, sizes, heads, planes)
    if planes:
        below, beside = after((below, beside), known)
        second, below_beside = moved(below, up(shards)), moved(below, cross(shards))
        own_far, below_far, beside_far = (
            moved(part, core(shards)) for part in (own, below, beside)
        )
        light_query, light_key = after((light_query, light_key), table)
    weights, faded_k, faded_q = local_part(
        light_query, light_key, log_decay, seg_col, seg_row, group
    )
    if planes:
        second, below_beside, weights, faded_k, faded_q = after(
            (second, below_beside, weights, faded_k, faded_q)
        )
        last = moved(second, cross(shards))
        second_far, below_beside_far, last_far = (
            moved(part, core(shards)) for part in (second, below_beside, last)
        )
        pieces = [below, second, beside, below_beside, last, own_far, below_far, second_far]
        pieces += [beside_far, below_beside_far, last_far]

    attended = None

    def attend(chunk, turn, attended):
        return attend_part(
            whiches[chunk * kv_chunk + turn],
            table,
            biases,
            sparse_query,
            own,
            faded_k,
            pieces,
            sizes,
            kv_chunk,
            attended,
        )

    if planes:
        attended, send0 = attend(0, 0, attended)
        attended, keep0 = attend(0, 1, attended)
        carry0 = carried_in_planes(keep0, send0, passing, place, shards, 0, heads)
        attended = after(attended, next(carry0))
        attended, send1 = attend(1, 0, attended)
        attended = after(attended, next(carry0))
        attended, keep1 = attend(1, 1, attended)
        inside = inside_part(weights, attended, group)
        carry1 = carried_in_planes(keep1, send1, passing, place, shards, head_chunk, heads)
        next(carry1)
        next(carry1)
        states = [carry0.send(inside), carry1.send(None)]
    else:
        parts = []
        for kv_head in range(kv_heads):
            attended, state = attend(0, kv_head, attended)
            parts.append(state)
        inside = inside_part(weights, attended, group)
        entering = carried_in_any(jnp.concatenate(parts), passing[:, :heads], me, shards)
        entering = entering * passing[me, heads].astype(BF16)
        states = [(entering, entering)]
    result, squares = output_part(place, inside, faded_q, states, group, planes)
    if lax.axis_size("head") == 2:
        squares = squares + lax.ppermute(squares, "head", [(0, 1), (1, 0)])
    else:
        squares = lax.psum(squares, "head")
    return (attended, scale_part(squares, result, group))


def solution(mesh):
    in_specs = (
        P("seq", "head"),
        P("seq", "head"),
        P("seq", "head"),
        P("seq", "head"),
        P("seq", "head"),
        P("head", "seq"),
        P("seq"),
        P("seq", None),
    )
    out_specs = (P("seq", "head"), P("seq", "head"))
    return jax.shard_map(body, mesh=mesh, in_specs=in_specs, out_specs=out_specs, check_vma=False)
```

```python
import functools

import jax
import jax.numpy as jnp
from jax import lax
from jax.experimental import pallas as pl
from jax.experimental.pallas import tpu as pltpu
from jax.sharding import PartitionSpec as P

ASKER_CHANNELS = 64
HD = 128
BLK = 128

NEG = -1e30
norm_eps = 1e-06
LOG2E = 1.4426950408889634
F32 = jnp.float32
BF16 = jnp.bfloat16
CLASSES = (1, 2, 3, 5, 7, 9)


def room(mib):
    return pltpu.CompilerParams(vmem_limit_bytes=mib * 1024 * 1024)


def far(value):
    return pltpu.with_memory_space_constraint(value, pltpu.HBM)


def nt(a, b):
    return lax.dot_general(a, b, (((1,), (1,)), ((), ())), preferred_element_type=F32)


def tn(a, b):
    return lax.dot_general(a, b, (((0,), (0,)), ((), ())), preferred_element_type=F32)


def nn(a, b):
    return lax.dot_general(a, b, (((1,), (0,)), ((), ())), preferred_element_type=F32)


def info_kernel(decay_ref, seg_ref, info_ref):
    rows, lanes = info_ref.shape
    heads, tokens = decay_ref.shape
    ones = jnp.ones((rows, tokens), F32)
    totals = lax.dot_general(
        ones,
        decay_ref[...],
        (((1,), (1,)), ((), ())),
        precision=lax.Precision.HIGHEST,
        preferred_element_type=F32,
    )
    info_ref[...] = jnp.zeros((rows, lanes), F32)
    info_ref[:, :heads] = totals
    seg = seg_ref[...]
    for doc in range(1, 4):
        count = jnp.sum((seg < doc).astype(F32), axis=1, keepdims=True)
        info_ref[:, heads + doc - 1 : heads + doc] = jnp.broadcast_to(count, (rows, 1))
    ends = seg.astype(F32)
    info_ref[:, heads + 3 : heads + 4] = jnp.broadcast_to(ends[:, :1], (rows, 1))
    info_ref[:, heads + 4 : heads + 5] = jnp.broadcast_to(ends[:, tokens - 1 :], (rows, 1))


def own_info(log_decay, seg_row, shards):
    return pl.pallas_call(
        info_kernel,
        out_shape=jax.ShapeDtypeStruct((shards, 128), F32),
        compiler_params=room(2),
        name="own_info",
    )(log_decay, seg_row)


def passing_kernel(heads, tokens, known_ref, passing_ref):
    known = known_ref[...]
    rows = known.shape[0]
    firsts, lasts = known[:, heads + 3 : heads + 4], known[:, heads + 4 : heads + 5]
    begins = jnp.zeros_like(firsts)
    for doc in range(1, 4):
        start = jnp.sum(known[:, heads + doc - 1 : heads + doc], axis=0, keepdims=True)
        begins = jnp.where(firsts == doc, start, begins)
    position = lax.broadcasted_iota(jnp.int32, (rows, 1), 0) * tokens
    begun = begins < position.astype(F32)
    through = begun & (firsts == lasts)
    lane = lax.broadcasted_iota(jnp.int32, known.shape, 1)
    decay = jnp.exp(jnp.where(lane < heads, known, 0.0))
    passing_ref[...] = jnp.where(lane == heads, begun.astype(F32), jnp.where(through, decay, 0.0))


def all_passing(known, heads, tokens):
    return pl.pallas_call(
        functools.partial(passing_kernel, heads, tokens),
        out_shape=jax.ShapeDtypeStruct(known.shape, F32),
        compiler_params=room(2),
        name="passing",
    )(known)


def local_kernel(q_ref, k_ref, decay_ref, segc_ref, segr_ref, w_ref, kf_ref, qf_ref, bias, upper):
    tokens = q_ref.shape[0]

    @pl.when(pl.program_id(0) == 0)
    def _():
        t = lax.broadcasted_iota(jnp.int32, (tokens, tokens), 0)
        s = lax.broadcasted_iota(jnp.int32, (tokens, tokens), 1)
        seen = (s <= t) & (segc_ref[...] == segr_ref[...])
        bias[...] = jnp.where(seen, 0.0, NEG)
        upper[...] = (t <= s).astype(F32)

    row = lax.dot_general(
        decay_ref[...],
        upper[...],
        (((1,), (0,)), ((), ())),
        precision=lax.Precision.HIGHEST,
        preferred_element_type=F32,
    )
    seg = segc_ref[...]
    col = jnp.transpose(row)
    fade = jnp.where(seg == seg[tokens - 1 :, :], jnp.exp(col[tokens - 1 :, :] - col), 0.0)
    reach = jnp.where(seg == seg[:1, :], jnp.exp(col), 0.0)
    for i in range(w_ref.shape[0]):
        cols = slice(i * HD, (i + 1) * HD)
        k = k_ref[:, cols]
        q = q_ref[:, cols]
        spread = col[:, i : i + 1] - row[i : i + 1, :]
        w_ref[i] = (nt(q, k) * jnp.exp(spread + bias[...])).astype(BF16)
        kf_ref[i] = jnp.transpose((k.astype(F32) * fade[:, i : i + 1]).astype(BF16))
        qf_ref[:, cols] = (q.astype(F32) * reach[:, i : i + 1]).astype(BF16)


def local_part(light_q, light_k, log_decay, seg_col, seg_row, per_step):
    tokens, width = light_q.shape
    heads = width // HD
    steps = heads // per_step
    wide = pl.BlockSpec((tokens, per_step * HD), lambda g: (0, g))
    return pl.pallas_call(
        local_kernel,
        grid=(steps,),
        in_specs=[
            wide,
            wide,
            pl.BlockSpec((per_step, tokens), lambda g: (g, 0)),
            pl.BlockSpec((tokens, 1), lambda g: (0, 0)),
            pl.BlockSpec((1, tokens), lambda g: (0, 0)),
        ],
        out_specs=[
            pl.BlockSpec((per_step, tokens, tokens), lambda g: (g, 0, 0)),
            pl.BlockSpec((per_step, HD, tokens), lambda g: (g, 0, 0)),
            wide,
        ],
        out_shape=[
            jax.ShapeDtypeStruct((heads, tokens, tokens), BF16),
            jax.ShapeDtypeStruct((heads, HD, tokens), BF16),
            jax.ShapeDtypeStruct((tokens, width), BF16),
        ],
        scratch_shapes=[pltpu.VMEM((tokens, tokens), F32), pltpu.VMEM((tokens, tokens), F32)],
        compiler_params=room(14),
        cost_estimate=pl.CostEstimate(
            flops=2 * heads * tokens * tokens * HD,
            bytes_accessed=4 * 2 * tokens * width + 2 * heads * tokens * tokens,
            transcendentals=heads * tokens * tokens,
        ),
        name="local_scores",
    )(far(light_q), far(light_k), log_decay, seg_col, seg_row)


def table_kernel(sizes, planes, heads, listing, known, place_ref, segc_ref, segr_ref, *refs):
    own_bias, row_bias, key_bias, table, named, counts = refs
    tokens = segc_ref.shape[0]
    blocks = tokens // BLK
    shards = known.shape[0]
    per_row = listing.shape[0] // blocks
    total = sum(sizes)
    me = place_ref[0]
    first_doc = known[me, heads + 3].astype(jnp.int32)
    begin = known[0, heads] * 0.0
    for doc in range(1, 4):
        start = known[0, heads + doc - 1]
        for j in range(1, shards):
            start = start + known[j, heads + doc - 1]
        begin = jnp.where(first_doc == doc, start, begin)
    begin = begin.astype(jnp.int32)
    for delta in range(shards):
        named[delta] = 0
    for b in range(blocks):
        counts[b] = 0
    for e in range(listing.shape[0]):
        entry = listing[e]
        delta = jnp.where(entry >= 0, me - lax.div(jnp.maximum(entry, 0), blocks), 0)
        named[delta] = 1 + (e // per_row) * blocks + lax.rem(jnp.maximum(entry, 0), blocks)
    named[0] = 0
    key_bias[...] = jnp.full(key_bias.shape, NEG, F32)
    lane = lax.broadcasted_iota(jnp.int32, (BLK, BLK), 1)
    sub = lax.broadcasted_iota(jnp.int32, (BLK, BLK), 0)
    for b in range(blocks):
        here = slice(b * BLK, (b + 1) * BLK)
        ok = (lane <= sub) & (segc_ref[here, :] == segr_ref[:, here])
        own_bias[b] = jnp.where(ok, 0.0, NEG)
        ok = jnp.broadcast_to(segc_ref[here, :], (BLK, BLK)) == first_doc
        row_bias[b] = jnp.where(ok, 0.0, NEG)

    def fill(slot, owner, usable):
        usable = usable & (owner >= 0) & (owner < me)
        code = named[jnp.where(usable, me - owner, 0)] - 1
        half = lax.rem(jnp.maximum(code, 0), blocks)
        least = begin - (owner * blocks + half) * BLK
        seen = usable & (code >= 0) & (least < BLK)
        b = lax.div(jnp.maximum(code, 0), blocks)
        to = jnp.where(seen, counts[b] + 1, 0)
        table[3 * slot] = b * (1 + per_row) + to
        table[3 * slot + 1] = half
        table[3 * slot + 2] = seen.astype(jnp.int32)

        @pl.when(seen)
        def _():
            counts[b] = to
            at = b * (1 + per_row) + to
            key_bias[pl.ds(at, 1)] = jnp.where(lane[:8] >= least, 0.0, NEG)[None]

    if planes:
        for slot, (owner, usable) in enumerate(window_owners(me)):
            fill(slot, owner, usable)
    else:

        def fill_step(j, carry):
            fill(j, j, j >= 0)
            return carry

        lax.fori_loop(0, shards, fill_step, 0)
    for b in range(blocks):
        table[3 * total + b] = counts[b]


def seen_table(place, listing, known, seg_col, seg_row, sizes, heads, planes):
    blocks = seg_col.shape[0] // BLK
    tiles = listing.shape[0] + blocks
    smem = pl.BlockSpec(memory_space=pltpu.SMEM)
    vmem = pl.BlockSpec(memory_space=pltpu.VMEM)
    return pl.pallas_call(
        functools.partial(table_kernel, sizes, planes, heads),
        in_specs=[smem, smem, smem, vmem, vmem],
        out_specs=[vmem, vmem, vmem, smem],
        out_shape=[
            jax.ShapeDtypeStruct((blocks, BLK, BLK), F32),
            jax.ShapeDtypeStruct((blocks, BLK, BLK), F32),
            jax.ShapeDtypeStruct((tiles, 8, BLK), F32),
            jax.ShapeDtypeStruct((3 * sum(sizes) + blocks,), jnp.int32),
        ],
        scratch_shapes=[
            pltpu.SMEM((known.shape[0],), jnp.int32),
            pltpu.SMEM((blocks,), jnp.int32),
        ],
        compiler_params=room(6),
        name="seen_table",
    )(listing, known, place, seg_col, seg_row)


def attend_kernel(sizes, shifts, kv_step, group, kv_head, table, *refs):
    pieces = len(sizes)
    query_ref, own_ref, kf_ref, own_bias, row_bias, key_bias = refs[:6]
    piece = refs[6 : 6 + pieces]
    out_ref, state_ref, q_ref, keys, values, sems, q_sems = refs[-7:]
    tokens, width = out_ref.shape
    blocks = tokens // BLK
    first_head = kv_head[0] * group
    per_row = keys.shape[0] // (blocks * BLK) - 1
    factor = HD ** (-0.5) * LOG2E
    total = sum(sizes)

    def each_piece(do):
        at = 0
        for i, size in enumerate(sizes):
            if size == 1:
                do(i, at, 0)
            else:

                def step(j, carry, i=i, at=at):
                    do(i, at + j, j)
                    return carry

                lax.fori_loop(0, size, step, 0)
            at += size

    def copies(i, slot, j):
        span = pl.ds(pl.multiple_of(j * tokens + table[3 * slot + 1] * BLK, BLK), BLK)
        to = pl.ds(pl.multiple_of(table[3 * slot] * BLK, BLK), BLK)
        for part, buffer in enumerate((keys, values)):
            col = kv_head[1] + part * kv_step - shifts[i]
            cols = pl.ds(pl.multiple_of(col * HD, HD), HD)
            yield pltpu.make_async_copy(piece[i].at[span, cols], buffer.at[to, :], sems.at[part, slot])

    def bring(i, slot, j):
        @pl.when(table[3 * slot + 2] > 0)
        def _():
            for copy in copies(i, slot, j):
                copy.start()

    def arrive(i, slot, j):
        @pl.when(table[3 * slot + 2] > 0)
        def _():
            for copy in copies(i, slot, j):
                copy.wait()

    def query_copy(b):
        here = pl.ds(pl.multiple_of(b * BLK, BLK), BLK)
        cols = pl.ds(pl.multiple_of(kv_head[0] * width, HD), width)
        return pltpu.make_async_copy(query_ref.at[here, cols], q_ref.at[here, :], q_sems.at[b])

    for b in range(blocks):
        query_copy(b).start()
    each_piece(bring)
    for b in range(blocks):
        base = b * (1 + per_row) * BLK
        for part, buffer in enumerate((keys, values)):
            cols = pl.ds(pl.multiple_of((kv_head[1] + part * kv_step) * HD, HD), HD)
            buffer[base : base + BLK, :] = own_ref[b * BLK : (b + 1) * BLK, cols]
    each_piece(arrive)

    def heads_out(b, tiles, h, count):
        base = b * (1 + per_row)
        here = pl.ds(pl.multiple_of(b * BLK, BLK), BLK)
        span = pl.ds(pl.multiple_of(base * BLK, BLK), tiles * BLK)
        cols = [pl.ds(pl.multiple_of((h + j) * HD, HD), HD) for j in range(count)]
        query = jnp.concatenate([q_ref[here, c] for c in cols], axis=0)
        score = nt(query, keys[span, :]).reshape(count, BLK, tiles * BLK)
        bias = [own_bias[b]] + [row_bias[b] + key_bias[base + t][:1, :] for t in range(1, tiles)]
        score = score + jnp.concatenate(bias, axis=1)[None]
        lifted = jnp.exp2((score - jnp.max(score, axis=2, keepdims=True)) * factor)
        weight = lifted * (1.0 / jnp.sum(lifted, axis=2, keepdims=True))
        weight = weight.astype(BF16).reshape(count * BLK, tiles * BLK)
        result = nn(weight, values[span, :]).astype(BF16)
        for j, c in enumerate(cols):
            out_ref[here, c] = result[j * BLK : (j + 1) * BLK, :]

    classes = sorted({min(t, 1 + per_row) for t in CLASSES} | {1 + per_row})

    def block_out(b, carry):
        query_copy(b).wait()
        need = table[3 * total + b] + 1
        low = 0
        for tiles in classes:
            together = min(group, 8 if tiles <= 2 else 4 if tiles <= 5 else 2)

            @pl.when((need > low) & (need <= tiles))
            def _(low=low, tiles=tiles, together=together):
                for t in range(max(low + 1, 1), tiles):

                    @pl.when(t >= need)
                    def _(t=t):
                        start = pl.multiple_of((b * (1 + per_row) + t) * BLK, BLK)
                        keys[pl.ds(start, BLK), :] = jnp.zeros((BLK, HD), BF16)
                        values[pl.ds(start, BLK), :] = jnp.zeros((BLK, HD), BF16)

                def step(i, carry):
                    heads_out(b, tiles, i * together, together)
                    return carry

                lax.fori_loop(0, group // together, step, 0)

            low = tiles
        return carry

    lax.fori_loop(0, blocks, block_out, 0)
    for h in range(group):
        state_ref[h] = nn(kf_ref[first_head + h], out_ref[:, h * HD : (h + 1) * HD])


def attend_part(
    kv_head, table, biases, query, own, faded, pieces, sizes, shifts, kv_step
):
    tokens = query.shape[0]
    group = faded.shape[0] * HD // own.shape[1] * 2
    blocks = tokens // BLK
    smem = pl.BlockSpec(memory_space=pltpu.SMEM)
    vmem = pl.BlockSpec(memory_space=pltpu.VMEM)
    anywhere = pl.BlockSpec(memory_space=pl.ANY)
    rows = biases[2].shape[0] * BLK
    return pl.pallas_call(
        functools.partial(attend_kernel, sizes, shifts, kv_step, group),
        in_specs=[smem, smem, anywhere] + [vmem] * 5 + [anywhere] * len(pieces),
        out_specs=[vmem, vmem],
        scratch_shapes=[
            pltpu.VMEM((tokens, group * HD), BF16),
            pltpu.VMEM((rows, HD), BF16),
            pltpu.VMEM((rows, HD), BF16),
            pltpu.SemaphoreType.DMA((2, sum(sizes))),
            pltpu.SemaphoreType.DMA((blocks,)),
        ],
        out_shape=[
            jax.ShapeDtypeStruct((tokens, group * HD), BF16),
            jax.ShapeDtypeStruct((group, HD, HD), F32),
        ],
        compiler_params=room(12),
        cost_estimate=pl.CostEstimate(
            flops=group * 10 * 6 * BLK * BLK * HD,
            bytes_accessed=12 * 4 * query.shape[0] * HD,
            transcendentals=group * 10 * BLK * BLK,
        ),
        name="attend",
    )(kv_head, table, query, own, faded, *biases, *pieces)


def inside_kernel(calls, order, w_ref, *refs):
    part_refs = refs[:calls]
    out_ref, whole_ref, sems = refs[calls:]
    width = part_refs[0].shape[1]
    group = width // HD

    def copy(i):
        cols = pl.ds(pl.multiple_of(order[i] * width, HD), width)
        return pltpu.make_async_copy(part_refs[i], whole_ref.at[:, cols], sems.at[i])

    for i in range(calls):
        copy(i).start()
    for i in range(calls):
        for h in range(group):
            at = order[i] * group + h
            cols = pl.ds(pl.multiple_of(at * HD, HD), HD)
            out_ref[:, cols] = nn(w_ref[at], part_refs[i][:, h * HD : (h + 1) * HD])
    for i in range(calls):
        copy(i).wait()


def inside_part(order, weights, parts):
    tokens = weights.shape[1]
    width = weights.shape[0] * HD
    vmem = pl.BlockSpec(memory_space=pltpu.VMEM)
    return pl.pallas_call(
        functools.partial(inside_kernel, len(parts)),
        in_specs=[pl.BlockSpec(memory_space=pltpu.SMEM)] + [vmem] * (1 + len(parts)),
        out_specs=[vmem, pl.BlockSpec(memory_space=pl.ANY)],
        out_shape=[
            jax.ShapeDtypeStruct((tokens, width), F32),
            jax.ShapeDtypeStruct((tokens, width), BF16),
        ],
        scratch_shapes=[pltpu.SemaphoreType.DMA((len(parts),))],
        compiler_params=room(4),
        cost_estimate=pl.CostEstimate(
            flops=width * 2 * tokens * tokens,
            bytes_accessed=2 * tokens * tokens * (width // HD) + 6 * tokens * width,
            transcendentals=0,
        ),
        name="inside",
    )(order, weights, *parts)


def output_kernel(planes, group, place_ref, q_ref, inside_ref, *refs):
    out_ref, squares_ref = refs[-2:]
    states = refs[:-2]
    keeps, gots = states[: len(states) // 2], states[len(states) // 2 :]
    tokens, width = out_ref.shape
    per = width // HD // group // len(keeps)

    def part(first, state_of, total):
        for i in range(group):
            cols = slice((first + i) * HD, (first + i + 1) * HD)
            result = inside_ref[:, cols] + nn(q_ref[:, cols], state_of(i))
            out_ref[:, cols] = result
            total += result * result
        return total

    total = jnp.zeros((tokens, HD), F32)
    for chunk, (keep_ref, got_ref) in enumerate(zip(keeps, gots, strict=True)):
        for g in range(per):
            first = (chunk * per + g) * group
            if planes:
                mine = (place_ref[0] & 1) == g
                total = part(first, lambda i: jnp.where(mine, keep_ref[i], got_ref[i]), total)
            else:
                total = part(first, lambda i: keep_ref[g * group + i], total)
    squares_ref[...] = jnp.sum(jnp.transpose(total), axis=0, keepdims=True)


def output_part(place, inside, faded_q, states, group, planes):
    tokens, width = faded_q.shape
    smem = pl.BlockSpec(memory_space=pltpu.SMEM)
    vmem = pl.BlockSpec(memory_space=pltpu.VMEM)
    return pl.pallas_call(
        functools.partial(output_kernel, planes, group),
        in_specs=[smem] + [vmem] * (2 + 2 * len(states)),
        out_specs=[vmem, vmem],
        out_shape=[
            jax.ShapeDtypeStruct((tokens, width), F32),
            jax.ShapeDtypeStruct((1, tokens), F32),
        ],
        input_output_aliases={2: 0},
        compiler_params=room(4),
        cost_estimate=pl.CostEstimate(
            flops=2 * tokens * width * HD,
            bytes_accessed=10 * tokens * width + 2 * width * HD,
            transcendentals=0,
        ),
        name="outputs",
    )(place, faded_q, inside, *[k for k, _ in states], *[g for _, g in states])


def scale_kernel(features, squares_ref, value_ref, out_ref, buffer, sems):
    tokens, width = value_ref.shape
    row = lax.rsqrt(squares_ref[...] / features + norm_eps)
    scale = jnp.transpose(jnp.broadcast_to(row, (HD, tokens)))
    parts = sems.shape[0]
    span = width // parts

    def copy(part):
        cols = slice(part * span, (part + 1) * span)
        return pltpu.make_async_copy(buffer.at[:, cols], out_ref.at[:, cols], sems.at[part])

    for part in range(parts):
        for i in range(span // HD):
            cols = slice(part * span + i * HD, part * span + (i + 1) * HD)
            buffer[:, cols] = (value_ref[:, cols] * scale).astype(BF16)
        copy(part).start()
    for part in range(parts):
        copy(part).wait()


def scale_part(squares, value, parts):
    tokens, width = value.shape
    vmem = pl.BlockSpec(memory_space=pltpu.VMEM)
    return pl.pallas_call(
        functools.partial(scale_kernel, ASKER_CHANNELS * HD),
        in_specs=[vmem, vmem],
        out_specs=pl.BlockSpec(memory_space=pl.ANY),
        out_shape=jax.ShapeDtypeStruct((tokens, width), BF16),
        scratch_shapes=[pltpu.VMEM((tokens, width), BF16), pltpu.SemaphoreType.DMA((parts,))],
        compiler_params=room(6),
        name="scaled",
    )(squares, value)


def moved(value, pairs):
    return lax.ppermute(value, "seq", pairs)


def up(shards):
    return [(i, (i + 4) % shards) for i in range(shards)]


def cross(shards):
    return [(i, i ^ 2) for i in range(shards)]


def core(shards):
    return [(i, i ^ 1) for i in range(shards)]


def after(values, *first):
    return lax.optimization_barrier((values, first))[0]


def window_owners(me):
    always = me >= 0
    right, left = (me & 2) > 0, (me & 2) == 0

    def seen_from(at):
        side = at ^ 2
        return [
            (at - 4, always),
            (at - 8, always),
            (side, right),
            (side - 4, always),
            (side - 8, left),
        ]

    return seen_from(me) + [(me ^ 1, always)] + seen_from(me ^ 1)


def mixing_kernel(body, passing, place_ref, *refs):
    me = place_ref[0]
    body(passing, me, me & 1, (me >> 1) & 1, *refs)


def mixing(name, body, passing, place, values, outs):
    smem = pl.BlockSpec(memory_space=pltpu.SMEM)
    vmem = pl.BlockSpec(memory_space=pltpu.VMEM)
    return pl.pallas_call(
        functools.partial(mixing_kernel, body),
        in_specs=[smem, smem] + [vmem] * len(values),
        out_specs=[vmem] * len(outs),
        out_shape=[jax.ShapeDtypeStruct((n, HD, HD), dtype) for n, dtype in outs],
        cost_estimate=pl.CostEstimate(
            flops=4 * sum(n for n, _ in outs) * HD * HD,
            bytes_accessed=8 * sum(n for n, _ in outs) * HD * HD,
            transcendentals=0,
        ),
        compiler_params=room(4),
        name=name,
    )(passing, place, *values)


def carried_in_planes(keep, send, passing, place, shards, head0, heads):
    half = keep.shape[0]
    quarter = half // 2
    def chip_body(passing, me, c, x, keep_ref, far_ref, near_ref, send_ref):
        base = head0 + c * half
        for part, to in ((x, near_ref), (1 - x, send_ref)):
            for i in range(quarter):
                h = part * quarter + i
                fade = passing[me | 1, base + h]
                a, b = jnp.where(c == 0, fade, 1.0), jnp.where(c == 0, 1.0, fade)
                to[i] = (keep_ref[h] * a + far_ref[h] * b).astype(to.dtype)

    def plane_body(passing, me, c, x, near_ref, far_ref, out_ref):
        base = head0 + c * half + x * quarter
        for i in range(quarter):
            fade = passing[me | 3, base + i] * passing[(me | 3) - 1, base + i]
            a, b = jnp.where(x == 0, fade, 1.0), jnp.where(x == 0, 1.0, fade)
            out_ref[i] = (near_ref[i] * a + far_ref[i].astype(F32) * b).astype(BF16)

    def enter_body(passing, me, c, x, near_ref, far_ref, one_ref, two_ref, keep_ref, send_ref):
        base = head0 + c * half + x * quarter
        plane = me & ~3
        low = jnp.maximum(plane - 4, 0)
        for i in range(quarter):
            h = base + i
            fade = passing[low, h] * passing[low + 1, h] * passing[low + 2, h] * passing[low + 3, h]
            e0 = jnp.where(me >= 4, one_ref[i].astype(F32), 0.0)
            e0 = jnp.where(me >= 8, e0 + two_ref[i].astype(F32) * fade, e0)
            chip = jnp.where(x == 0, near_ref[i], far_ref[i].astype(F32))
            e1 = e0 * (passing[plane, h] * passing[plane + 1, h]) + chip
            keep_ref[i] = jnp.where(x == 0, e0, e1)
            send_ref[i] = jnp.where(x == 0, e1, e0).astype(BF16)

    def core_body(passing, me, c, x, keep_ref, far_ref, near_ref, got_ref, mine_ref, send_ref):
        base = head0 + c * half
        mine_on, other_on = passing[me, heads], passing[me ^ 1, heads]
        for part, source in ((x, near_ref), (1 - x, got_ref)):
            for i in range(quarter):
                h = part * quarter + i
                e0 = source[i].astype(F32)
                first = jnp.where(c == 0, keep_ref[h], far_ref[h])
                e1 = e0 * passing[me & ~1, base + h] + first
                mine_ref[h] = (jnp.where(c == 0, e0, e1) * mine_on).astype(BF16)
                send_ref[h] = (jnp.where(c == 0, e1, e0) * other_on).astype(BF16)

    sent = moved(send, core(shards))
    near_q, send_q = mixing(
        "mix_chip", chip_body, passing, place, [keep, sent], [(quarter, F32), (quarter, BF16)]
    )
    far_q = moved(send_q, cross(shards))
    yield send_q
    (plane_state,) = mixing(
        "mix_plane", plane_body, passing, place, [near_q, far_q], [(quarter, BF16)]
    )
    one_below = moved(plane_state, up(shards))
    wait = yield plane_state
    if wait is not None:
        near_q = after(near_q, wait)
    two_below = moved(one_below, up(shards))
    near_e, send_e = mixing(
        "mix_enter",
        enter_body,
        passing,
        place,
        [near_q, far_q, one_below, two_below],
        [(quarter, F32), (quarter, BF16)],
    )
    got_e = moved(send_e, cross(shards))
    mine, other = mixing(
        "mix_core", core_body, passing, place, [keep, sent, near_e, got_e], [(half, BF16), (half, BF16)]
    )
    yield mine, moved(other, core(shards))


def carried_in_any(state, passing, me, shards):
    states = lax.all_gather(state, "seq")

    def turn(j, total):
        part = passing[j][:, None, None] * total + states[j].astype(F32)
        return jnp.where(j < me, part, total)

    return lax.fori_loop(0, shards, turn, jnp.zeros(state.shape, F32)).astype(BF16)


def body(
    sparse_query, sparse_key, sparse_value, light_query, light_key, log_decay, segments, block_list
):
    tokens = sparse_query.shape[0]
    kv_heads = sparse_key.shape[1] // HD
    heads = light_query.shape[1] // HD
    group = heads // kv_heads
    shards = lax.axis_size("seq")
    me = lax.axis_index("seq")
    place = me.astype(jnp.int32).reshape(1)
    planes = shards == 16 and kv_heads == 4
    chunks = 2 if planes else 1
    kv_chunk = kv_heads // chunks
    head_chunk = heads // chunks
    parts = []
    for chunk in range(chunks):
        cols = slice(chunk * kv_chunk * HD, (chunk + 1) * kv_chunk * HD)
        parts += [sparse_key[:, cols], sparse_value[:, cols]]
    own = jnp.concatenate(parts, axis=1)
    seg_col, seg_row, listing = segments[:, None], segments[None, :], block_list.reshape(-1)
    if planes:
        below, beside = moved(own, up(shards)), moved(own, cross(shards))
    else:
        pieces = [lax.all_gather(own, "seq", axis=0, tiled=True)]
    whiches = []
    for chunk in range(chunks):
        turns = [1 - (me & 1), me & 1] if planes else range(kv_chunk)
        for kv_head in turns:
            kv_head = jnp.asarray(kv_head, jnp.int32)
            at = [chunk * kv_chunk + kv_head, chunk * 2 * kv_chunk + kv_head]
            whiches.append(jnp.stack(at))
    order = jnp.stack([which[0] for which in whiches])
    info = own_info(log_decay, seg_row, shards)
    info, whiches, order, place, listing, seg_col = after(
        (info, whiches, order, place, listing, seg_col), own
    )
    known = lax.all_to_all(info, "seq", 0, 0, tiled=True)
    passing = all_passing(known, heads, tokens)
    sizes = (1,) * 11 if planes else (shards,)
    *biases, table = seen_table(place, listing, known, seg_col, seg_row, sizes, heads, planes)
    if planes:
        below, beside = after((below, beside), known)
        second, below_beside = moved(below, up(shards)), moved(below, cross(shards))
        own_far, below_far, beside_far = (
            moved(part, core(shards)) for part in (own, below, beside)
        )
        light_query, light_key = after((light_query, light_key), table)
    weights, faded_k, faded_q = local_part(
        light_query, light_key, log_decay, seg_col, seg_row, group
    )
    if planes:
        second, below_beside, weights, faded_k, faded_q = after(
            (second, below_beside, weights, faded_k, faded_q)
        )
        span = own.shape[1] // 2
        lasts = [
            moved(second[:, :span], cross(shards)),
            moved(below_beside[:, span:], up(shards)),
        ]
        lasts = after(lasts)
        second_far, below_beside_far = (
            moved(part, core(shards)) for part in (second, below_beside)
        )
        last_fars = [moved(last, core(shards)) for last in lasts]
        pieces = [below, second, beside, below_beside, lasts, own_far, below_far, second_far]
        pieces += [beside_far, below_beside_far, last_fars]

    def attend(turn, first=None):
        which = whiches[turn] if first is None else after(whiches[turn], first)
        chunk = turn // kv_chunk
        mine = [p[chunk] if isinstance(p, list) else p for p in pieces]
        shifts = [chunk * 2 * kv_chunk if isinstance(p, list) else 0 for p in pieces]
        return attend_part(
            which, table, biases, sparse_query, own, faded_k, mine, sizes, shifts, kv_chunk
        )

    if planes:
        part0, send0 = attend(0)
        part1, keep0 = attend(1, part0)
        carry0 = carried_in_planes(keep0, send0, passing, place, shards, 0, heads)
        part2, send1 = attend(2, next(carry0))
        next(carry0)
        part3, keep1 = attend(3, part2)
        inside, attended = inside_part(order, weights, [part0, part1, part2, part3])
        carry1 = carried_in_planes(keep1, send1, passing, place, shards, head_chunk, heads)
        next(carry1)
        next(carry1)
        states = [carry0.send(inside), carry1.send(None)]
    else:
        parts, found = zip(*[attend(turn) for turn in range(kv_heads)], strict=True)
        inside, attended = inside_part(order, weights, parts)
        entering = carried_in_any(jnp.concatenate(found), passing[:, :heads], me, shards)
        entering = entering * passing[me, heads].astype(BF16)
        states = [(entering, entering)]
    result, squares = output_part(place, inside, faded_q, states, group, planes)
    if lax.axis_size("head") == 2:
        squares = squares + lax.ppermute(squares, "head", [(0, 1), (1, 0)])
    else:
        squares = lax.psum(squares, "head")
    return (attended, scale_part(squares, result, 8))


def solution(mesh):
    in_specs = (
        P("seq", "head"),
        P("seq", "head"),
        P("seq", "head"),
        P("seq", "head"),
        P("seq", "head"),
        P("head", "seq"),
        P("seq"),
        P("seq", None),
    )
    out_specs = (P("seq", "head"), P("seq", "head"))
    return jax.shard_map(body, mesh=mesh, in_specs=in_specs, out_specs=out_specs, check_vma=False)
```

```python
import functools

import jax
import jax.numpy as jnp
from jax import lax
from jax.experimental import pallas as pl
from jax.experimental.pallas import tpu as pltpu
from jax.sharding import PartitionSpec as P

ASKER_CHANNELS = 64
HD = 128
BLK = 128

NEG = -1e30
norm_eps = 1e-06
LOG2E = 1.4426950408889634
F32 = jnp.float32
BF16 = jnp.bfloat16
CLASSES = (1, 2, 3, 5, 7, 9)


def room(mib):
    return pltpu.CompilerParams(vmem_limit_bytes=mib * 1024 * 1024)


def far(value):
    return pltpu.with_memory_space_constraint(value, pltpu.HBM)


def nt(a, b):
    return lax.dot_general(a, b, (((1,), (1,)), ((), ())), preferred_element_type=F32)


def tn(a, b):
    return lax.dot_general(a, b, (((0,), (0,)), ((), ())), preferred_element_type=F32)


def nn(a, b):
    return lax.dot_general(a, b, (((1,), (0,)), ((), ())), preferred_element_type=F32)


def info_kernel(decay_ref, seg_ref, info_ref):
    rows, lanes = info_ref.shape
    heads, tokens = decay_ref.shape
    ones = jnp.ones((rows, tokens), F32)
    totals = lax.dot_general(
        ones,
        decay_ref[...],
        (((1,), (1,)), ((), ())),
        precision=lax.Precision.HIGHEST,
        preferred_element_type=F32,
    )
    info_ref[...] = jnp.zeros((rows, lanes), F32)
    info_ref[:, :heads] = totals
    seg = seg_ref[...]
    for doc in range(1, 4):
        count = jnp.sum((seg < doc).astype(F32), axis=1, keepdims=True)
        info_ref[:, heads + doc - 1 : heads + doc] = jnp.broadcast_to(count, (rows, 1))
    ends = seg.astype(F32)
    info_ref[:, heads + 3 : heads + 4] = jnp.broadcast_to(ends[:, :1], (rows, 1))
    info_ref[:, heads + 4 : heads + 5] = jnp.broadcast_to(ends[:, tokens - 1 :], (rows, 1))


def own_info(log_decay, seg_row, shards):
    return pl.pallas_call(
        info_kernel,
        out_shape=jax.ShapeDtypeStruct((shards, 128), F32),
        compiler_params=room(2),
        name="own_info",
    )(log_decay, seg_row)


def passing_kernel(heads, tokens, known_ref, passing_ref):
    known = known_ref[...]
    rows = known.shape[0]
    firsts, lasts = known[:, heads + 3 : heads + 4], known[:, heads + 4 : heads + 5]
    begins = jnp.zeros_like(firsts)
    for doc in range(1, 4):
        start = jnp.sum(known[:, heads + doc - 1 : heads + doc], axis=0, keepdims=True)
        begins = jnp.where(firsts == doc, start, begins)
    position = lax.broadcasted_iota(jnp.int32, (rows, 1), 0) * tokens
    begun = begins < position.astype(F32)
    through = begun & (firsts == lasts)
    lane = lax.broadcasted_iota(jnp.int32, known.shape, 1)
    decay = jnp.exp(jnp.where(lane < heads, known, 0.0))
    passing_ref[...] = jnp.where(lane == heads, begun.astype(F32), jnp.where(through, decay, 0.0))


def all_passing(known, heads, tokens):
    return pl.pallas_call(
        functools.partial(passing_kernel, heads, tokens),
        out_shape=jax.ShapeDtypeStruct(known.shape, F32),
        compiler_params=room(2),
        name="passing",
    )(known)


def local_kernel(q_ref, k_ref, decay_ref, segc_ref, segr_ref, w_ref, kf_ref, qf_ref, bias, upper):
    tokens = q_ref.shape[0]

    @pl.when(pl.program_id(0) == 0)
    def _():
        t = lax.broadcasted_iota(jnp.int32, (tokens, tokens), 0)
        s = lax.broadcasted_iota(jnp.int32, (tokens, tokens), 1)
        seen = (s <= t) & (segc_ref[...] == segr_ref[...])
        bias[...] = jnp.where(seen, 0.0, NEG)
        upper[...] = (t <= s).astype(F32)

    row = lax.dot_general(
        decay_ref[...],
        upper[...],
        (((1,), (0,)), ((), ())),
        precision=lax.Precision.HIGHEST,
        preferred_element_type=F32,
    )
    seg = segc_ref[...]
    col = jnp.transpose(row)
    fade = jnp.where(seg == seg[tokens - 1 :, :], jnp.exp(col[tokens - 1 :, :] - col), 0.0)
    reach = jnp.where(seg == seg[:1, :], jnp.exp(col), 0.0)
    for i in range(w_ref.shape[0]):
        cols = slice(i * HD, (i + 1) * HD)
        k = k_ref[:, cols]
        q = q_ref[:, cols]
        spread = col[:, i : i + 1] - row[i : i + 1, :]
        w_ref[i] = (nt(q, k) * jnp.exp(spread + bias[...])).astype(BF16)
        kf_ref[i] = jnp.transpose((k.astype(F32) * fade[:, i : i + 1]).astype(BF16))
        qf_ref[:, cols] = (q.astype(F32) * reach[:, i : i + 1]).astype(BF16)


def local_part(light_q, light_k, log_decay, seg_col, seg_row, per_step):
    tokens, width = light_q.shape
    heads = width // HD
    steps = heads // per_step
    wide = pl.BlockSpec((tokens, per_step * HD), lambda g: (0, g))
    return pl.pallas_call(
        local_kernel,
        grid=(steps,),
        in_specs=[
            wide,
            wide,
            pl.BlockSpec((per_step, tokens), lambda g: (g, 0)),
            pl.BlockSpec((tokens, 1), lambda g: (0, 0)),
            pl.BlockSpec((1, tokens), lambda g: (0, 0)),
        ],
        out_specs=[
            pl.BlockSpec((per_step, tokens, tokens), lambda g: (g, 0, 0)),
            pl.BlockSpec((per_step, HD, tokens), lambda g: (g, 0, 0)),
            wide,
        ],
        out_shape=[
            jax.ShapeDtypeStruct((heads, tokens, tokens), BF16),
            jax.ShapeDtypeStruct((heads, HD, tokens), BF16),
            jax.ShapeDtypeStruct((tokens, width), BF16),
        ],
        scratch_shapes=[pltpu.VMEM((tokens, tokens), F32), pltpu.VMEM((tokens, tokens), F32)],
        compiler_params=room(14),
        cost_estimate=pl.CostEstimate(
            flops=2 * heads * tokens * tokens * HD,
            bytes_accessed=4 * 2 * tokens * width + 2 * heads * tokens * tokens,
            transcendentals=heads * tokens * tokens,
        ),
        name="local_scores",
    )(far(light_q), far(light_k), log_decay, seg_col, seg_row)


def table_kernel(sizes, planes, heads, listing, known, place_ref, segc_ref, segr_ref, *refs):
    own_bias, row_bias, key_bias, table, named, counts = refs
    tokens = segc_ref.shape[0]
    blocks = tokens // BLK
    shards = known.shape[0]
    per_row = listing.shape[0] // blocks
    total = sum(sizes)
    me = place_ref[0]
    first_doc = known[me, heads + 3].astype(jnp.int32)
    begin = known[0, heads] * 0.0
    for doc in range(1, 4):
        start = known[0, heads + doc - 1]
        for j in range(1, shards):
            start = start + known[j, heads + doc - 1]
        begin = jnp.where(first_doc == doc, start, begin)
    begin = begin.astype(jnp.int32)
    for delta in range(shards):
        named[delta] = 0
    for b in range(blocks):
        counts[b] = 0
    for e in range(listing.shape[0]):
        entry = listing[e]
        delta = jnp.where(entry >= 0, me - lax.div(jnp.maximum(entry, 0), blocks), 0)
        named[delta] = 1 + (e // per_row) * blocks + lax.rem(jnp.maximum(entry, 0), blocks)
    named[0] = 0
    key_bias[...] = jnp.full(key_bias.shape, NEG, F32)
    lane = lax.broadcasted_iota(jnp.int32, (BLK, BLK), 1)
    sub = lax.broadcasted_iota(jnp.int32, (BLK, BLK), 0)
    for b in range(blocks):
        here = slice(b * BLK, (b + 1) * BLK)
        ok = (lane <= sub) & (segc_ref[here, :] == segr_ref[:, here])
        own_bias[b] = jnp.where(ok, 0.0, NEG)
        ok = jnp.broadcast_to(segc_ref[here, :], (BLK, BLK)) == first_doc
        row_bias[b] = jnp.where(ok, 0.0, NEG)

    def fill(slot, owner, usable):
        usable = usable & (owner >= 0) & (owner < me)
        code = named[jnp.where(usable, me - owner, 0)] - 1
        half = lax.rem(jnp.maximum(code, 0), blocks)
        least = begin - (owner * blocks + half) * BLK
        seen = usable & (code >= 0) & (least < BLK)
        b = lax.div(jnp.maximum(code, 0), blocks)
        to = jnp.where(seen, counts[b] + 1, 0)
        table[3 * slot] = b * (1 + per_row) + to
        table[3 * slot + 1] = half
        table[3 * slot + 2] = seen.astype(jnp.int32)

        @pl.when(seen)
        def _():
            counts[b] = to
            at = b * (1 + per_row) + to
            key_bias[pl.ds(at, 1)] = jnp.where(lane[:8] >= least, 0.0, NEG)[None]

    if planes:
        for slot, (owner, usable) in enumerate(window_owners(me)):
            fill(slot, owner, usable)
    else:

        def fill_step(j, carry):
            fill(j, j, j >= 0)
            return carry

        lax.fori_loop(0, shards, fill_step, 0)
    for b in range(blocks):
        table[3 * total + b] = counts[b]


def seen_table(place, listing, known, seg_col, seg_row, sizes, heads, planes):
    blocks = seg_col.shape[0] // BLK
    tiles = listing.shape[0] + blocks
    smem = pl.BlockSpec(memory_space=pltpu.SMEM)
    vmem = pl.BlockSpec(memory_space=pltpu.VMEM)
    return pl.pallas_call(
        functools.partial(table_kernel, sizes, planes, heads),
        in_specs=[smem, smem, smem, vmem, vmem],
        out_specs=[vmem, vmem, vmem, smem],
        out_shape=[
            jax.ShapeDtypeStruct((blocks, BLK, BLK), F32),
            jax.ShapeDtypeStruct((blocks, BLK, BLK), F32),
            jax.ShapeDtypeStruct((tiles, 8, BLK), F32),
            jax.ShapeDtypeStruct((3 * sum(sizes) + blocks,), jnp.int32),
        ],
        scratch_shapes=[
            pltpu.SMEM((known.shape[0],), jnp.int32),
            pltpu.SMEM((blocks,), jnp.int32),
        ],
        compiler_params=room(6),
        name="seen_table",
    )(listing, known, place, seg_col, seg_row)


def attend_kernel(sizes, shifts, kv_step, group, kv_head, table, *refs):
    pieces = len(sizes)
    query_ref, own_ref, kf_ref, own_bias, row_bias, key_bias = refs[:6]
    piece = refs[6 : 6 + pieces]
    out_ref, state_ref, q_ref, keys, values, sems, q_sems = refs[-7:]
    tokens, width = out_ref.shape
    blocks = tokens // BLK
    first_head = kv_head[0] * group
    per_row = keys.shape[0] // (blocks * BLK) - 1
    factor = HD ** (-0.5) * LOG2E
    total = sum(sizes)

    def each_piece(do):
        at = 0
        for i, size in enumerate(sizes):
            if size == 1:
                do(i, at, 0)
            else:

                def step(j, carry, i=i, at=at):
                    do(i, at + j, j)
                    return carry

                lax.fori_loop(0, size, step, 0)
            at += size

    def copies(i, slot, j):
        span = pl.ds(pl.multiple_of(j * tokens + table[3 * slot + 1] * BLK, BLK), BLK)
        to = pl.ds(pl.multiple_of(table[3 * slot] * BLK, BLK), BLK)
        for part, buffer in enumerate((keys, values)):
            col = kv_head[1] + part * kv_step - shifts[i]
            cols = pl.ds(pl.multiple_of(col * HD, HD), HD)
            yield pltpu.make_async_copy(piece[i].at[span, cols], buffer.at[to, :], sems.at[part, slot])

    def bring(i, slot, j):
        @pl.when(table[3 * slot + 2] > 0)
        def _():
            for copy in copies(i, slot, j):
                copy.start()

    def arrive(i, slot, j):
        @pl.when(table[3 * slot + 2] > 0)
        def _():
            for copy in copies(i, slot, j):
                copy.wait()

    def query_copy(b):
        here = pl.ds(pl.multiple_of(b * BLK, BLK), BLK)
        cols = pl.ds(pl.multiple_of(kv_head[0] * width, HD), width)
        return pltpu.make_async_copy(query_ref.at[here, cols], q_ref.at[here, :], q_sems.at[b])

    for b in range(blocks):
        query_copy(b).start()
    each_piece(bring)
    for b in range(blocks):
        base = b * (1 + per_row) * BLK
        for part, buffer in enumerate((keys, values)):
            cols = pl.ds(pl.multiple_of((kv_head[1] + part * kv_step) * HD, HD), HD)
            buffer[base : base + BLK, :] = own_ref[b * BLK : (b + 1) * BLK, cols]
    each_piece(arrive)

    def heads_out(b, tiles, h, count):
        base = b * (1 + per_row)
        here = pl.ds(pl.multiple_of(b * BLK, BLK), BLK)
        span = pl.ds(pl.multiple_of(base * BLK, BLK), tiles * BLK)
        cols = [pl.ds(pl.multiple_of((h + j) * HD, HD), HD) for j in range(count)]
        query = jnp.concatenate([q_ref[here, c] for c in cols], axis=0)
        score = nt(query, keys[span, :]).reshape(count, BLK, tiles * BLK)
        bias = [own_bias[b]] + [row_bias[b] + key_bias[base + t][:1, :] for t in range(1, tiles)]
        score = score + jnp.concatenate(bias, axis=1)[None]
        lifted = jnp.exp2((score - jnp.max(score, axis=2, keepdims=True)) * factor)
        weight = lifted * (1.0 / jnp.sum(lifted, axis=2, keepdims=True))
        weight = weight.astype(BF16).reshape(count * BLK, tiles * BLK)
        result = nn(weight, values[span, :]).astype(BF16)
        for j, c in enumerate(cols):
            out_ref[here, c] = result[j * BLK : (j + 1) * BLK, :]

    classes = sorted({min(t, 1 + per_row) for t in CLASSES} | {1 + per_row})

    def block_out(b, carry):
        query_copy(b).wait()
        need = table[3 * total + b] + 1
        low = 0
        for tiles in classes:
            together = min(group, 8 if tiles <= 2 else 4 if tiles <= 5 else 2)

            @pl.when((need > low) & (need <= tiles))
            def _(low=low, tiles=tiles, together=together):
                for t in range(max(low + 1, 1), tiles):

                    @pl.when(t >= need)
                    def _(t=t):
                        start = pl.multiple_of((b * (1 + per_row) + t) * BLK, BLK)
                        keys[pl.ds(start, BLK), :] = jnp.zeros((BLK, HD), BF16)
                        values[pl.ds(start, BLK), :] = jnp.zeros((BLK, HD), BF16)

                def step(i, carry):
                    heads_out(b, tiles, i * together, together)
                    return carry

                lax.fori_loop(0, group // together, step, 0)

            low = tiles
        return carry

    lax.fori_loop(0, blocks, block_out, 0)
    for h in range(group):
        state_ref[h] = nn(kf_ref[first_head + h], out_ref[:, h * HD : (h + 1) * HD])


def attend_part(
    kv_head, table, biases, query, own, faded, pieces, sizes, shifts, kv_step
):
    tokens = query.shape[0]
    group = faded.shape[0] * HD // own.shape[1] * 2
    blocks = tokens // BLK
    smem = pl.BlockSpec(memory_space=pltpu.SMEM)
    vmem = pl.BlockSpec(memory_space=pltpu.VMEM)
    anywhere = pl.BlockSpec(memory_space=pl.ANY)
    rows = biases[2].shape[0] * BLK
    return pl.pallas_call(
        functools.partial(attend_kernel, sizes, shifts, kv_step, group),
        in_specs=[smem, smem, anywhere] + [vmem] * 5 + [anywhere] * len(pieces),
        out_specs=[vmem, vmem],
        scratch_shapes=[
            pltpu.VMEM((tokens, group * HD), BF16),
            pltpu.VMEM((rows, HD), BF16),
            pltpu.VMEM((rows, HD), BF16),
            pltpu.SemaphoreType.DMA((2, sum(sizes))),
            pltpu.SemaphoreType.DMA((blocks,)),
        ],
        out_shape=[
            jax.ShapeDtypeStruct((tokens, group * HD), BF16),
            jax.ShapeDtypeStruct((group, HD, HD), F32),
        ],
        compiler_params=room(12),
        cost_estimate=pl.CostEstimate(
            flops=group * 10 * 6 * BLK * BLK * HD * 10,
            bytes_accessed=12 * 4 * query.shape[0] * HD * 10,
            transcendentals=group * 10 * BLK * BLK,
        ),
        name="attend",
    )(kv_head, table, query, own, faded, *biases, *pieces)


def inside_kernel(calls, order, w_ref, *refs):
    part_refs = refs[:calls]
    out_ref, whole_ref, sems = refs[calls:]
    width = part_refs[0].shape[1]
    group = width // HD

    def copy(i):
        cols = pl.ds(pl.multiple_of(order[i] * width, HD), width)
        return pltpu.make_async_copy(part_refs[i], whole_ref.at[:, cols], sems.at[i])

    for i in range(calls):
        copy(i).start()
    for i in range(calls):
        for h in range(group):
            at = order[i] * group + h
            cols = pl.ds(pl.multiple_of(at * HD, HD), HD)
            out_ref[:, cols] = nn(w_ref[at], part_refs[i][:, h * HD : (h + 1) * HD])
    for i in range(calls):
        copy(i).wait()


def inside_part(order, weights, parts):
    tokens = weights.shape[1]
    width = weights.shape[0] * HD
    vmem = pl.BlockSpec(memory_space=pltpu.VMEM)
    return pl.pallas_call(
        functools.partial(inside_kernel, len(parts)),
        in_specs=[pl.BlockSpec(memory_space=pltpu.SMEM)] + [vmem] * (1 + len(parts)),
        out_specs=[vmem, pl.BlockSpec(memory_space=pl.ANY)],
        out_shape=[
            jax.ShapeDtypeStruct((tokens, width), F32),
            jax.ShapeDtypeStruct((tokens, width), BF16),
        ],
        scratch_shapes=[pltpu.SemaphoreType.DMA((len(parts),))],
        compiler_params=room(4),
        cost_estimate=pl.CostEstimate(
            flops=width * 2 * tokens * tokens,
            bytes_accessed=2 * tokens * tokens * (width // HD) + 6 * tokens * width,
            transcendentals=0,
        ),
        name="inside",
    )(order, weights, *parts)


def output_kernel(planes, group, place_ref, q_ref, inside_ref, *refs):
    out_ref, squares_ref = refs[-2:]
    states = refs[:-2]
    keeps, gots = states[: len(states) // 2], states[len(states) // 2 :]
    tokens, width = out_ref.shape
    per = width // HD // group // len(keeps)

    def part(first, state_of, total):
        for i in range(group):
            cols = slice((first + i) * HD, (first + i + 1) * HD)
            result = inside_ref[:, cols] + nn(q_ref[:, cols], state_of(i))
            out_ref[:, cols] = result
            total += result * result
        return total

    total = jnp.zeros((tokens, HD), F32)
    for chunk, (keep_ref, got_ref) in enumerate(zip(keeps, gots, strict=True)):
        for g in range(per):
            first = (chunk * per + g) * group
            if planes:
                mine = (place_ref[0] & 1) == g
                total = part(first, lambda i: jnp.where(mine, keep_ref[i], got_ref[i]), total)
            else:
                total = part(first, lambda i: keep_ref[g * group + i], total)
    squares_ref[...] = jnp.sum(jnp.transpose(total), axis=0, keepdims=True)


def output_part(place, inside, faded_q, states, group, planes):
    tokens, width = faded_q.shape
    smem = pl.BlockSpec(memory_space=pltpu.SMEM)
    vmem = pl.BlockSpec(memory_space=pltpu.VMEM)
    return pl.pallas_call(
        functools.partial(output_kernel, planes, group),
        in_specs=[smem] + [vmem] * (2 + 2 * len(states)),
        out_specs=[vmem, vmem],
        out_shape=[
            jax.ShapeDtypeStruct((tokens, width), F32),
            jax.ShapeDtypeStruct((1, tokens), F32),
        ],
        input_output_aliases={2: 0},
        compiler_params=room(4),
        cost_estimate=pl.CostEstimate(
            flops=2 * tokens * width * HD,
            bytes_accessed=10 * tokens * width + 2 * width * HD,
            transcendentals=0,
        ),
        name="outputs",
    )(place, faded_q, inside, *[k for k, _ in states], *[g for _, g in states])


def scale_kernel(features, squares_ref, value_ref, out_ref, buffer, sems):
    tokens, width = value_ref.shape
    row = lax.rsqrt(squares_ref[...] / features + norm_eps)
    scale = jnp.transpose(jnp.broadcast_to(row, (HD, tokens)))
    parts = sems.shape[0]
    span = width // parts

    def copy(part):
        cols = slice(part * span, (part + 1) * span)
        return pltpu.make_async_copy(buffer.at[:, cols], out_ref.at[:, cols], sems.at[part])

    for part in range(parts):
        for i in range(span // HD):
            cols = slice(part * span + i * HD, part * span + (i + 1) * HD)
            buffer[:, cols] = (value_ref[:, cols] * scale).astype(BF16)
        copy(part).start()
    for part in range(parts):
        copy(part).wait()


def scale_part(squares, value, parts):
    tokens, width = value.shape
    vmem = pl.BlockSpec(memory_space=pltpu.VMEM)
    return pl.pallas_call(
        functools.partial(scale_kernel, ASKER_CHANNELS * HD),
        in_specs=[vmem, vmem],
        out_specs=pl.BlockSpec(memory_space=pl.ANY),
        out_shape=jax.ShapeDtypeStruct((tokens, width), BF16),
        scratch_shapes=[pltpu.VMEM((tokens, width), BF16), pltpu.SemaphoreType.DMA((parts,))],
        compiler_params=room(6),
        name="scaled",
    )(squares, value)


def moved(value, pairs):
    return lax.ppermute(value, "seq", pairs)


def up(shards):
    return [(i, (i + 4) % shards) for i in range(shards)]


def cross(shards):
    return [(i, i ^ 2) for i in range(shards)]


def core(shards):
    return [(i, i ^ 1) for i in range(shards)]


def after(values, *first):
    return lax.optimization_barrier((values, first))[0]


def window_owners(me):
    always = me >= 0
    right, left = (me & 2) > 0, (me & 2) == 0

    def seen_from(at):
        side = at ^ 2
        return [
            (at - 4, always),
            (at - 8, always),
            (side, right),
            (side - 4, always),
            (side - 8, left),
        ]

    return seen_from(me) + [(me ^ 1, always)] + seen_from(me ^ 1)


def mixing_kernel(body, passing, place_ref, *refs):
    me = place_ref[0]
    body(passing, me, me & 1, (me >> 1) & 1, *refs)


def mixing(name, body, passing, place, values, outs):
    smem = pl.BlockSpec(memory_space=pltpu.SMEM)
    vmem = pl.BlockSpec(memory_space=pltpu.VMEM)
    return pl.pallas_call(
        functools.partial(mixing_kernel, body),
        in_specs=[smem, smem] + [vmem] * len(values),
        out_specs=[vmem] * len(outs),
        out_shape=[jax.ShapeDtypeStruct((n, HD, HD), dtype) for n, dtype in outs],
        cost_estimate=pl.CostEstimate(
            flops=4 * sum(n for n, _ in outs) * HD * HD,
            bytes_accessed=8 * sum(n for n, _ in outs) * HD * HD,
            transcendentals=0,
        ),
        compiler_params=room(4),
        name=name,
    )(passing, place, *values)


def carried_in_planes(keep, send, passing, place, shards, head0, heads):
    half = keep.shape[0]
    quarter = half // 2
    def chip_body(passing, me, c, x, keep_ref, far_ref, near_ref, send_ref):
        base = head0 + c * half
        for part, to in ((x, near_ref), (1 - x, send_ref)):
            for i in range(quarter):
                h = part * quarter + i
                fade = passing[me | 1, base + h]
                a, b = jnp.where(c == 0, fade, 1.0), jnp.where(c == 0, 1.0, fade)
                to[i] = (keep_ref[h] * a + far_ref[h] * b).astype(to.dtype)

    def plane_body(passing, me, c, x, near_ref, far_ref, out_ref):
        base = head0 + c * half + x * quarter
        for i in range(quarter):
            fade = passing[me | 3, base + i] * passing[(me | 3) - 1, base + i]
            a, b = jnp.where(x == 0, fade, 1.0), jnp.where(x == 0, 1.0, fade)
            out_ref[i] = (near_ref[i] * a + far_ref[i].astype(F32) * b).astype(BF16)

    def enter_body(passing, me, c, x, near_ref, far_ref, one_ref, two_ref, keep_ref, send_ref):
        base = head0 + c * half + x * quarter
        plane = me & ~3
        low = jnp.maximum(plane - 4, 0)
        for i in range(quarter):
            h = base + i
            fade = passing[low, h] * passing[low + 1, h] * passing[low + 2, h] * passing[low + 3, h]
            e0 = jnp.where(me >= 4, one_ref[i].astype(F32), 0.0)
            e0 = jnp.where(me >= 8, e0 + two_ref[i].astype(F32) * fade, e0)
            chip = jnp.where(x == 0, near_ref[i], far_ref[i].astype(F32))
            e1 = e0 * (passing[plane, h] * passing[plane + 1, h]) + chip
            keep_ref[i] = jnp.where(x == 0, e0, e1)
            send_ref[i] = jnp.where(x == 0, e1, e0).astype(BF16)

    def core_body(passing, me, c, x, keep_ref, far_ref, near_ref, got_ref, mine_ref, send_ref):
        base = head0 + c * half
        mine_on, other_on = passing[me, heads], passing[me ^ 1, heads]
        for part, source in ((x, near_ref), (1 - x, got_ref)):
            for i in range(quarter):
                h = part * quarter + i
                e0 = source[i].astype(F32)
                first = jnp.where(c == 0, keep_ref[h], far_ref[h])
                e1 = e0 * passing[me & ~1, base + h] + first
                mine_ref[h] = (jnp.where(c == 0, e0, e1) * mine_on).astype(BF16)
                send_ref[h] = (jnp.where(c == 0, e1, e0) * other_on).astype(BF16)

    sent = moved(send, core(shards))
    near_q, send_q = mixing(
        "mix_chip", chip_body, passing, place, [keep, sent], [(quarter, F32), (quarter, BF16)]
    )
    far_q = moved(send_q, cross(shards))
    wait = yield send_q
    near_q = near_q if wait is None else after(near_q, wait)
    (plane_state,) = mixing(
        "mix_plane", plane_body, passing, place, [near_q, far_q], [(quarter, BF16)]
    )
    one_below = moved(plane_state, up(shards))
    yield plane_state, one_below
    two_below = moved(one_below, up(shards))
    wait = yield two_below
    near_q = near_q if wait is None else after(near_q, wait)
    near_e, send_e = mixing(
        "mix_enter",
        enter_body,
        passing,
        place,
        [near_q, far_q, one_below, two_below],
        [(quarter, F32), (quarter, BF16)],
    )
    got_e = moved(send_e, cross(shards))
    yield got_e
    mine, other = mixing(
        "mix_core", core_body, passing, place, [keep, sent, near_e, got_e], [(half, BF16), (half, BF16)]
    )
    yield mine, moved(other, core(shards))


def carried_in_any(state, passing, me, shards):
    states = lax.all_gather(state, "seq")

    def turn(j, total):
        part = passing[j][:, None, None] * total + states[j].astype(F32)
        return jnp.where(j < me, part, total)

    return lax.fori_loop(0, shards, turn, jnp.zeros(state.shape, F32)).astype(BF16)


def body(
    sparse_query, sparse_key, sparse_value, light_query, light_key, log_decay, segments, block_list
):
    tokens = sparse_query.shape[0]
    kv_heads = sparse_key.shape[1] // HD
    heads = light_query.shape[1] // HD
    group = heads // kv_heads
    shards = lax.axis_size("seq")
    me = lax.axis_index("seq")
    place = me.astype(jnp.int32).reshape(1)
    planes = shards == 16 and kv_heads == 4
    chunks = 2 if planes else 1
    kv_chunk = kv_heads // chunks
    head_chunk = heads // chunks
    parts = []
    for chunk in range(chunks):
        cols = slice(chunk * kv_chunk * HD, (chunk + 1) * kv_chunk * HD)
        parts += [sparse_key[:, cols], sparse_value[:, cols]]
    own = jnp.concatenate(parts, axis=1)
    seg_col, seg_row, listing = segments[:, None], segments[None, :], block_list.reshape(-1)
    if planes:
        beside = moved(own, cross(shards))
        below = moved(own, up(shards))
    else:
        pieces = [lax.all_gather(own, "seq", axis=0, tiled=True)]
    whiches = []
    for chunk in range(chunks):
        turns = [1 - (me & 1), me & 1] if planes else range(kv_chunk)
        for kv_head in turns:
            kv_head = jnp.asarray(kv_head, jnp.int32)
            at = [chunk * kv_chunk + kv_head, chunk * 2 * kv_chunk + kv_head]
            whiches.append(jnp.stack(at))
    order = jnp.stack([which[0] for which in whiches])
    info = own_info(log_decay, seg_row, shards)
    info, whiches, order, place, listing, seg_col = after(
        (info, whiches, order, place, listing, seg_col), own
    )
    known = lax.all_to_all(info, "seq", 0, 0, tiled=True)
    passing = all_passing(known, heads, tokens)
    sizes = (1,) * 11 if planes else (shards,)
    *biases, table = seen_table(place, listing, known, seg_col, seg_row, sizes, heads, planes)
    if planes:
        beside, below = after((beside, below), known)
        below_beside = moved(below, cross(shards))
        second = moved(below, up(shards))
        own_far, below_far, beside_far = (
            moved(part, core(shards)) for part in (own, below, beside)
        )
        light_query, light_key = after((light_query, light_key), table)
    weights, faded_k, faded_q = local_part(
        light_query, light_key, log_decay, seg_col, seg_row, group
    )
    if planes:
        below_beside, second, weights, faded_k, faded_q = after(
            (below_beside, second, weights, faded_k, faded_q)
        )
        span = own.shape[1] // 2
        lasts = [moved(below_beside[:, span:], up(shards))]
        lasts.insert(0, moved(second[:, :span], cross(shards)))
        lasts = after(lasts)
        second_far, below_beside_far = (
            moved(part, core(shards)) for part in (second, below_beside)
        )
        last_fars = [moved(last, core(shards)) for last in lasts]
        pieces = [below, second, beside, below_beside, lasts, own_far, below_far, second_far]
        pieces += [beside_far, below_beside_far, last_fars]

    def attend(turn, first=None):
        which = whiches[turn] if first is None else after(whiches[turn], first)
        chunk = turn // kv_chunk
        mine = [p[chunk] if isinstance(p, list) else p for p in pieces]
        shifts = [chunk * 2 * kv_chunk if isinstance(p, list) else 0 for p in pieces]
        return attend_part(
            which, table, biases, sparse_query, own, faded_k, mine, sizes, shifts, kv_chunk
        )

    if planes:
        part0, send0 = attend(0)
        part1, keep0 = attend(1, part0)
        carry0 = carried_in_planes(keep0, send0, passing, place, shards, 0, heads)
        part2, send1 = attend(2, next(carry0))
        plane0, one0 = next(carry0)
        part3, keep1 = attend(3, (part2, plane0))
        next(carry0)
        keep1 = after(keep1, one0)
        carry1 = carried_in_planes(keep1, send1, passing, place, shards, head_chunk, heads)
        order = after(order, next(carry1))
        inside, attended = inside_part(order, weights, [part0, part1, part2, part3])
        got0 = next(carry0)
        carry1.send(inside)
        next(carry1)
        carry1.send(got0)
        states = [next(carry0), next(carry1)]
    else:
        parts, found = zip(*[attend(turn) for turn in range(kv_heads)], strict=True)
        inside, attended = inside_part(order, weights, parts)
        entering = carried_in_any(jnp.concatenate(found), passing[:, :heads], me, shards)
        entering = entering * passing[me, heads].astype(BF16)
        states = [(entering, entering)]
    result, squares = output_part(place, inside, faded_q, states, group, planes)
    if lax.axis_size("head") == 2:
        squares = squares + lax.ppermute(squares, "head", [(0, 1), (1, 0)])
    else:
        squares = lax.psum(squares, "head")
    return (attended, scale_part(squares, result, 8))


def solution(mesh):
    in_specs = (
        P("seq", "head"),
        P("seq", "head"),
        P("seq", "head"),
        P("seq", "head"),
        P("seq", "head"),
        P("head", "seq"),
        P("seq"),
        P("seq", None),
    )
    out_specs = (P("seq", "head"), P("seq", "head"))
    return jax.shard_map(body, mesh=mesh, in_specs=in_specs, out_specs=out_specs, check_vma=False)
```

```python
import functools

import jax
import jax.numpy as jnp
from jax import lax
from jax.experimental import pallas as pl
from jax.experimental.pallas import tpu as pltpu
from jax.sharding import PartitionSpec as P

ASKER_CHANNELS = 64
HD = 128
BLK = 128

NEG = -1e30
norm_eps = 1e-06
LOG2E = 1.4426950408889634
F32 = jnp.float32
BF16 = jnp.bfloat16
CLASSES = (1, 2, 3, 5, 7, 9)


def room(mib):
    return pltpu.CompilerParams(vmem_limit_bytes=mib * 1024 * 1024)


def far(value):
    return pltpu.with_memory_space_constraint(value, pltpu.HBM)


def nt(a, b):
    return lax.dot_general(a, b, (((1,), (1,)), ((), ())), preferred_element_type=F32)


def tn(a, b):
    return lax.dot_general(a, b, (((0,), (0,)), ((), ())), preferred_element_type=F32)


def nn(a, b):
    return lax.dot_general(a, b, (((1,), (0,)), ((), ())), preferred_element_type=F32)


def info_kernel(decay_ref, seg_ref, info_ref):
    rows, lanes = info_ref.shape
    heads, tokens = decay_ref.shape
    ones = jnp.ones((rows, tokens), F32)
    totals = lax.dot_general(
        ones,
        decay_ref[...],
        (((1,), (1,)), ((), ())),
        precision=lax.Precision.HIGHEST,
        preferred_element_type=F32,
    )
    info_ref[...] = jnp.zeros((rows, lanes), F32)
    info_ref[:, :heads] = totals
    seg = seg_ref[...]
    for doc in range(1, 4):
        count = jnp.sum((seg < doc).astype(F32), axis=1, keepdims=True)
        info_ref[:, heads + doc - 1 : heads + doc] = jnp.broadcast_to(count, (rows, 1))
    ends = seg.astype(F32)
    info_ref[:, heads + 3 : heads + 4] = jnp.broadcast_to(ends[:, :1], (rows, 1))
    info_ref[:, heads + 4 : heads + 5] = jnp.broadcast_to(ends[:, tokens - 1 :], (rows, 1))


def own_info(log_decay, seg_row, shards):
    return pl.pallas_call(
        info_kernel,
        out_shape=jax.ShapeDtypeStruct((shards, 128), F32),
        compiler_params=room(2),
        name="own_info",
    )(log_decay, seg_row)


def passing_kernel(heads, tokens, known_ref, passing_ref):
    known = known_ref[...]
    rows = known.shape[0]
    firsts, lasts = known[:, heads + 3 : heads + 4], known[:, heads + 4 : heads + 5]
    begins = jnp.zeros_like(firsts)
    for doc in range(1, 4):
        start = jnp.sum(known[:, heads + doc - 1 : heads + doc], axis=0, keepdims=True)
        begins = jnp.where(firsts == doc, start, begins)
    position = lax.broadcasted_iota(jnp.int32, (rows, 1), 0) * tokens
    begun = begins < position.astype(F32)
    through = begun & (firsts == lasts)
    lane = lax.broadcasted_iota(jnp.int32, known.shape, 1)
    decay = jnp.exp(jnp.where(lane < heads, known, 0.0))
    passing_ref[...] = jnp.where(lane == heads, begun.astype(F32), jnp.where(through, decay, 0.0))


def all_passing(known, heads, tokens):
    return pl.pallas_call(
        functools.partial(passing_kernel, heads, tokens),
        out_shape=jax.ShapeDtypeStruct(known.shape, F32),
        compiler_params=room(2),
        name="passing",
    )(known)


def local_kernel(q_ref, k_ref, decay_ref, segc_ref, segr_ref, w_ref, kf_ref, qf_ref, bias, upper):
    tokens = q_ref.shape[0]

    @pl.when(pl.program_id(0) == 0)
    def _():
        t = lax.broadcasted_iota(jnp.int32, (tokens, tokens), 0)
        s = lax.broadcasted_iota(jnp.int32, (tokens, tokens), 1)
        seen = (s <= t) & (segc_ref[...] == segr_ref[...])
        bias[...] = jnp.where(seen, 0.0, NEG)
        upper[...] = (t <= s).astype(F32)

    row = lax.dot_general(
        decay_ref[...],
        upper[...],
        (((1,), (0,)), ((), ())),
        precision=lax.Precision.HIGHEST,
        preferred_element_type=F32,
    )
    seg = segc_ref[...]
    col = jnp.transpose(row)
    fade = jnp.where(seg == seg[tokens - 1 :, :], jnp.exp(col[tokens - 1 :, :] - col), 0.0)
    reach = jnp.where(seg == seg[:1, :], jnp.exp(col), 0.0)
    for i in range(w_ref.shape[0]):
        cols = slice(i * HD, (i + 1) * HD)
        k = k_ref[:, cols]
        q = q_ref[:, cols]
        spread = col[:, i : i + 1] - row[i : i + 1, :]
        w_ref[i] = (nt(q, k) * jnp.exp(spread + bias[...])).astype(BF16)
        kf_ref[i] = jnp.transpose((k.astype(F32) * fade[:, i : i + 1]).astype(BF16))
        qf_ref[:, cols] = (q.astype(F32) * reach[:, i : i + 1]).astype(BF16)


def local_part(light_q, light_k, log_decay, seg_col, seg_row, per_step):
    tokens, width = light_q.shape
    heads = width // HD
    steps = heads // per_step
    wide = pl.BlockSpec((tokens, per_step * HD), lambda g: (0, g))
    return pl.pallas_call(
        local_kernel,
        grid=(steps,),
        in_specs=[
            wide,
            wide,
            pl.BlockSpec((per_step, tokens), lambda g: (g, 0)),
            pl.BlockSpec((tokens, 1), lambda g: (0, 0)),
            pl.BlockSpec((1, tokens), lambda g: (0, 0)),
        ],
        out_specs=[
            pl.BlockSpec((per_step, tokens, tokens), lambda g: (g, 0, 0)),
            pl.BlockSpec((per_step, HD, tokens), lambda g: (g, 0, 0)),
            wide,
        ],
        out_shape=[
            jax.ShapeDtypeStruct((heads, tokens, tokens), BF16),
            jax.ShapeDtypeStruct((heads, HD, tokens), BF16),
            jax.ShapeDtypeStruct((tokens, width), BF16),
        ],
        scratch_shapes=[pltpu.VMEM((tokens, tokens), F32), pltpu.VMEM((tokens, tokens), F32)],
        compiler_params=room(14),
        cost_estimate=pl.CostEstimate(
            flops=2 * heads * tokens * tokens * HD,
            bytes_accessed=4 * 2 * tokens * width + 2 * heads * tokens * tokens,
            transcendentals=heads * tokens * tokens,
        ),
        name="local_scores",
    )(far(light_q), far(light_k), log_decay, seg_col, seg_row)


def table_kernel(sizes, planes, heads, listing, known, place_ref, segc_ref, segr_ref, *refs):
    own_bias, row_bias, key_bias, table, named, counts = refs
    tokens = segc_ref.shape[0]
    blocks = tokens // BLK
    shards = known.shape[0]
    per_row = listing.shape[0] // blocks
    total = sum(sizes)
    me = place_ref[0]
    first_doc = known[me, heads + 3].astype(jnp.int32)
    begin = known[0, heads] * 0.0
    for doc in range(1, 4):
        start = known[0, heads + doc - 1]
        for j in range(1, shards):
            start = start + known[j, heads + doc - 1]
        begin = jnp.where(first_doc == doc, start, begin)
    begin = begin.astype(jnp.int32)
    for delta in range(shards):
        named[delta] = 0
    for b in range(blocks):
        counts[b] = 0
    for e in range(listing.shape[0]):
        entry = listing[e]
        delta = jnp.where(entry >= 0, me - lax.div(jnp.maximum(entry, 0), blocks), 0)
        named[delta] = 1 + (e // per_row) * blocks + lax.rem(jnp.maximum(entry, 0), blocks)
    named[0] = 0
    key_bias[...] = jnp.full(key_bias.shape, NEG, F32)
    lane = lax.broadcasted_iota(jnp.int32, (BLK, BLK), 1)
    sub = lax.broadcasted_iota(jnp.int32, (BLK, BLK), 0)
    for b in range(blocks):
        here = slice(b * BLK, (b + 1) * BLK)
        ok = (lane <= sub) & (segc_ref[here, :] == segr_ref[:, here])
        own_bias[b] = jnp.where(ok, 0.0, NEG)
        ok = jnp.broadcast_to(segc_ref[here, :], (BLK, BLK)) == first_doc
        row_bias[b] = jnp.where(ok, 0.0, NEG)

    def fill(slot, owner, usable):
        usable = usable & (owner >= 0) & (owner < me)
        code = named[jnp.where(usable, me - owner, 0)] - 1
        half = lax.rem(jnp.maximum(code, 0), blocks)
        least = begin - (owner * blocks + half) * BLK
        seen = usable & (code >= 0) & (least < BLK)
        b = lax.div(jnp.maximum(code, 0), blocks)
        to = jnp.where(seen, counts[b] + 1, 0)
        table[3 * slot] = b * (1 + per_row) + to
        table[3 * slot + 1] = half
        table[3 * slot + 2] = seen.astype(jnp.int32)

        @pl.when(seen)
        def _():
            counts[b] = to
            at = b * (1 + per_row) + to
            key_bias[pl.ds(at, 1)] = jnp.where(lane[:8] >= least, 0.0, NEG)[None]

    if planes:
        for slot, (owner, usable) in enumerate(window_owners(me)):
            fill(slot, owner, usable)
    else:

        def fill_step(j, carry):
            fill(j, j, j >= 0)
            return carry

        lax.fori_loop(0, shards, fill_step, 0)
    for b in range(blocks):
        table[3 * total + b] = counts[b]


def seen_table(place, listing, known, seg_col, seg_row, sizes, heads, planes):
    blocks = seg_col.shape[0] // BLK
    tiles = listing.shape[0] + blocks
    smem = pl.BlockSpec(memory_space=pltpu.SMEM)
    vmem = pl.BlockSpec(memory_space=pltpu.VMEM)
    return pl.pallas_call(
        functools.partial(table_kernel, sizes, planes, heads),
        in_specs=[smem, smem, smem, vmem, vmem],
        out_specs=[vmem, vmem, vmem, smem],
        out_shape=[
            jax.ShapeDtypeStruct((blocks, BLK, BLK), F32),
            jax.ShapeDtypeStruct((blocks, BLK, BLK), F32),
            jax.ShapeDtypeStruct((tiles, 8, BLK), F32),
            jax.ShapeDtypeStruct((3 * sum(sizes) + blocks,), jnp.int32),
        ],
        scratch_shapes=[
            pltpu.SMEM((known.shape[0],), jnp.int32),
            pltpu.SMEM((blocks,), jnp.int32),
        ],
        compiler_params=room(6),
        name="seen_table",
    )(listing, known, place, seg_col, seg_row)


def attend_kernel(sizes, shifts, kv_step, group, kv_head, table, *refs):
    pieces = len(sizes)
    query_ref, own_ref, kf_ref, own_bias, row_bias, key_bias = refs[:6]
    piece = refs[6 : 6 + pieces]
    out_ref, state_ref, q_ref, keys, values, sems, q_sems = refs[-7:]
    tokens, width = out_ref.shape
    blocks = tokens // BLK
    first_head = kv_head[0] * group
    per_row = keys.shape[0] // (blocks * BLK) - 1
    factor = HD ** (-0.5) * LOG2E
    total = sum(sizes)

    def each_piece(do):
        at = 0
        for i, size in enumerate(sizes):
            if size == 1:
                do(i, at, 0)
            else:

                def step(j, carry, i=i, at=at):
                    do(i, at + j, j)
                    return carry

                lax.fori_loop(0, size, step, 0)
            at += size

    def copies(i, slot, j):
        span = pl.ds(pl.multiple_of(j * tokens + table[3 * slot + 1] * BLK, BLK), BLK)
        to = pl.ds(pl.multiple_of(table[3 * slot] * BLK, BLK), BLK)
        for part, buffer in enumerate((keys, values)):
            col = kv_head[1] + part * kv_step - shifts[i]
            cols = pl.ds(pl.multiple_of(col * HD, HD), HD)
            yield pltpu.make_async_copy(piece[i].at[span, cols], buffer.at[to, :], sems.at[part, slot])

    def bring(i, slot, j):
        @pl.when(table[3 * slot + 2] > 0)
        def _():
            for copy in copies(i, slot, j):
                copy.start()

    def arrive(i, slot, j):
        @pl.when(table[3 * slot + 2] > 0)
        def _():
            for copy in copies(i, slot, j):
                copy.wait()

    def query_copy(b):
        here = pl.ds(pl.multiple_of(b * BLK, BLK), BLK)
        cols = pl.ds(pl.multiple_of(kv_head[0] * width, HD), width)
        return pltpu.make_async_copy(query_ref.at[here, cols], q_ref.at[here, :], q_sems.at[b])

    for b in range(blocks):
        query_copy(b).start()
    each_piece(bring)
    for b in range(blocks):
        base = b * (1 + per_row) * BLK
        for part, buffer in enumerate((keys, values)):
            cols = pl.ds(pl.multiple_of((kv_head[1] + part * kv_step) * HD, HD), HD)
            buffer[base : base + BLK, :] = own_ref[b * BLK : (b + 1) * BLK, cols]
    each_piece(arrive)

    def heads_out(b, tiles, h, count):
        base = b * (1 + per_row)
        here = pl.ds(pl.multiple_of(b * BLK, BLK), BLK)
        span = pl.ds(pl.multiple_of(base * BLK, BLK), tiles * BLK)
        cols = [pl.ds(pl.multiple_of((h + j) * HD, HD), HD) for j in range(count)]
        query = jnp.concatenate([q_ref[here, c] for c in cols], axis=0)
        score = nt(query, keys[span, :]).reshape(count, BLK, tiles * BLK)
        bias = [own_bias[b]] + [row_bias[b] + key_bias[base + t][:1, :] for t in range(1, tiles)]
        score = score + jnp.concatenate(bias, axis=1)[None]
        lifted = jnp.exp2((score - jnp.max(score, axis=2, keepdims=True)) * factor)
        weight = lifted * (1.0 / jnp.sum(lifted, axis=2, keepdims=True))
        weight = weight.astype(BF16).reshape(count * BLK, tiles * BLK)
        result = nn(weight, values[span, :]).astype(BF16)
        for j, c in enumerate(cols):
            out_ref[here, c] = result[j * BLK : (j + 1) * BLK, :]

    classes = sorted({min(t, 1 + per_row) for t in CLASSES} | {1 + per_row})

    def block_out(b, carry):
        query_copy(b).wait()
        need = table[3 * total + b] + 1
        low = 0
        for tiles in classes:
            together = min(group, 8 if tiles <= 2 else 4 if tiles <= 5 else 2)

            @pl.when((need > low) & (need <= tiles))
            def _(low=low, tiles=tiles, together=together):
                for t in range(max(low + 1, 1), tiles):

                    @pl.when(t >= need)
                    def _(t=t):
                        start = pl.multiple_of((b * (1 + per_row) + t) * BLK, BLK)
                        keys[pl.ds(start, BLK), :] = jnp.zeros((BLK, HD), BF16)
                        values[pl.ds(start, BLK), :] = jnp.zeros((BLK, HD), BF16)

                def step(i, carry):
                    heads_out(b, tiles, i * together, together)
                    return carry

                lax.fori_loop(0, group // together, step, 0)

            low = tiles
        return carry

    lax.fori_loop(0, blocks, block_out, 0)
    for h in range(group):
        state_ref[h] = nn(kf_ref[first_head + h], out_ref[:, h * HD : (h + 1) * HD])


def attend_part(
    kv_head, table, biases, query, own, faded, pieces, sizes, shifts, kv_step
):
    tokens = query.shape[0]
    group = faded.shape[0] * HD // own.shape[1] * 2
    blocks = tokens // BLK
    smem = pl.BlockSpec(memory_space=pltpu.SMEM)
    vmem = pl.BlockSpec(memory_space=pltpu.VMEM)
    anywhere = pl.BlockSpec(memory_space=pl.ANY)
    rows = biases[2].shape[0] * BLK
    return pl.pallas_call(
        functools.partial(attend_kernel, sizes, shifts, kv_step, group),
        in_specs=[smem, smem, anywhere] + [vmem] * 5 + [anywhere] * len(pieces),
        out_specs=[vmem, vmem],
        scratch_shapes=[
            pltpu.VMEM((tokens, group * HD), BF16),
            pltpu.VMEM((rows, HD), BF16),
            pltpu.VMEM((rows, HD), BF16),
            pltpu.SemaphoreType.DMA((2, sum(sizes))),
            pltpu.SemaphoreType.DMA((blocks,)),
        ],
        out_shape=[
            jax.ShapeDtypeStruct((tokens, group * HD), BF16),
            jax.ShapeDtypeStruct((group, HD, HD), F32),
        ],
        compiler_params=room(12),
        cost_estimate=pl.CostEstimate(
            flops=group * 10 * 6 * BLK * BLK * HD * 10,
            bytes_accessed=12 * 4 * query.shape[0] * HD * 10,
            transcendentals=group * 10 * BLK * BLK,
        ),
        name="attend",
    )(kv_head, table, query, own, faded, *biases, *pieces)


def inside_kernel(calls, order, w_ref, *refs):
    part_refs = refs[:calls]
    out_ref, whole_ref, sems = refs[calls:]
    width = part_refs[0].shape[1]
    group = width // HD

    def copy(i):
        cols = pl.ds(pl.multiple_of(order[i] * width, HD), width)
        return pltpu.make_async_copy(part_refs[i], whole_ref.at[:, cols], sems.at[i])

    for i in range(calls):
        copy(i).start()
    for i in range(calls):
        for h in range(group):
            at = order[i] * group + h
            cols = pl.ds(pl.multiple_of(at * HD, HD), HD)
            out_ref[:, cols] = nn(w_ref[at], part_refs[i][:, h * HD : (h + 1) * HD])
    for i in range(calls):
        copy(i).wait()


def inside_part(order, weights, parts):
    tokens = weights.shape[1]
    width = weights.shape[0] * HD
    vmem = pl.BlockSpec(memory_space=pltpu.VMEM)
    return pl.pallas_call(
        functools.partial(inside_kernel, len(parts)),
        in_specs=[pl.BlockSpec(memory_space=pltpu.SMEM)] + [vmem] * (1 + len(parts)),
        out_specs=[vmem, pl.BlockSpec(memory_space=pl.ANY)],
        out_shape=[
            jax.ShapeDtypeStruct((tokens, width), F32),
            jax.ShapeDtypeStruct((tokens, width), BF16),
        ],
        scratch_shapes=[pltpu.SemaphoreType.DMA((len(parts),))],
        compiler_params=room(4),
        cost_estimate=pl.CostEstimate(
            flops=width * 2 * tokens * tokens,
            bytes_accessed=2 * tokens * tokens * (width // HD) + 6 * tokens * width,
            transcendentals=0,
        ),
        name="inside",
    )(order, weights, *parts)


def output_kernel(planes, group, place_ref, q_ref, inside_ref, *refs):
    out_ref, squares_ref = refs[-2:]
    states = refs[:-2]
    keeps, gots = states[: len(states) // 2], states[len(states) // 2 :]
    tokens, width = out_ref.shape
    per = width // HD // group // len(keeps)

    def part(first, state_of, total):
        for i in range(group):
            cols = slice((first + i) * HD, (first + i + 1) * HD)
            result = inside_ref[:, cols] + nn(q_ref[:, cols], state_of(i))
            out_ref[:, cols] = result
            total += result * result
        return total

    total = jnp.zeros((tokens, HD), F32)
    for chunk, (keep_ref, got_ref) in enumerate(zip(keeps, gots, strict=True)):
        for g in range(per):
            first = (chunk * per + g) * group
            if planes:
                mine = (place_ref[0] & 1) == g
                total = part(first, lambda i: jnp.where(mine, keep_ref[i], got_ref[i]), total)
            else:
                total = part(first, lambda i: keep_ref[g * group + i], total)
    squares_ref[...] = jnp.sum(jnp.transpose(total), axis=0, keepdims=True)


def output_part(place, inside, faded_q, states, group, planes):
    tokens, width = faded_q.shape
    smem = pl.BlockSpec(memory_space=pltpu.SMEM)
    vmem = pl.BlockSpec(memory_space=pltpu.VMEM)
    return pl.pallas_call(
        functools.partial(output_kernel, planes, group),
        in_specs=[smem] + [vmem] * (2 + 2 * len(states)),
        out_specs=[vmem, vmem],
        out_shape=[
            jax.ShapeDtypeStruct((tokens, width), F32),
            jax.ShapeDtypeStruct((1, tokens), F32),
        ],
        input_output_aliases={2: 0},
        compiler_params=room(4),
        cost_estimate=pl.CostEstimate(
            flops=2 * tokens * width * HD,
            bytes_accessed=10 * tokens * width + 2 * width * HD,
            transcendentals=0,
        ),
        name="outputs",
    )(place, faded_q, inside, *[k for k, _ in states], *[g for _, g in states])


def scale_kernel(features, squares_ref, value_ref, out_ref, buffer, sems):
    tokens, width = value_ref.shape
    row = lax.rsqrt(squares_ref[...] / features + norm_eps)
    scale = jnp.transpose(jnp.broadcast_to(row, (HD, tokens)))
    parts = sems.shape[0]
    span = width // parts

    def copy(part):
        cols = slice(part * span, (part + 1) * span)
        return pltpu.make_async_copy(buffer.at[:, cols], out_ref.at[:, cols], sems.at[part])

    for part in range(parts):
        for i in range(span // HD):
            cols = slice(part * span + i * HD, part * span + (i + 1) * HD)
            buffer[:, cols] = (value_ref[:, cols] * scale).astype(BF16)
        copy(part).start()
    for part in range(parts):
        copy(part).wait()


def scale_part(squares, value, parts):
    tokens, width = value.shape
    vmem = pl.BlockSpec(memory_space=pltpu.VMEM)
    return pl.pallas_call(
        functools.partial(scale_kernel, ASKER_CHANNELS * HD),
        in_specs=[vmem, vmem],
        out_specs=pl.BlockSpec(memory_space=pl.ANY),
        out_shape=jax.ShapeDtypeStruct((tokens, width), BF16),
        scratch_shapes=[pltpu.VMEM((tokens, width), BF16), pltpu.SemaphoreType.DMA((parts,))],
        compiler_params=room(6),
        name="scaled",
    )(squares, value)


def moved(value, pairs):
    return lax.ppermute(value, "seq", pairs)


def up(shards):
    return [(i, (i + 4) % shards) for i in range(shards)]


def cross(shards):
    return [(i, i ^ 2) for i in range(shards)]


def core(shards):
    return [(i, i ^ 1) for i in range(shards)]


def after(values, *first):
    return lax.optimization_barrier((values, first))[0]


def window_owners(me):
    always = me >= 0
    right, left = (me & 2) > 0, (me & 2) == 0

    def seen_from(at):
        side = at ^ 2
        return [
            (at - 4, always),
            (at - 8, always),
            (side, right),
            (side - 4, always),
            (side - 8, left),
        ]

    return seen_from(me) + [(me ^ 1, always)] + seen_from(me ^ 1)


def mixing_kernel(body, passing, place_ref, *refs):
    me = place_ref[0]
    body(passing, me, me & 1, (me >> 1) & 1, *refs)


def mixing(name, body, passing, place, values, outs):
    smem = pl.BlockSpec(memory_space=pltpu.SMEM)
    vmem = pl.BlockSpec(memory_space=pltpu.VMEM)
    return pl.pallas_call(
        functools.partial(mixing_kernel, body),
        in_specs=[smem, smem] + [vmem] * len(values),
        out_specs=[vmem] * len(outs),
        out_shape=[jax.ShapeDtypeStruct((n, HD, HD), dtype) for n, dtype in outs],
        cost_estimate=pl.CostEstimate(
            flops=4 * sum(n for n, _ in outs) * HD * HD,
            bytes_accessed=8 * sum(n for n, _ in outs) * HD * HD,
            transcendentals=0,
        ),
        compiler_params=room(4),
        name=name,
    )(passing, place, *values)


def carried_in_planes(keep, send, passing, place, shards, head0, heads):
    half = keep.shape[0]
    quarter = half // 2
    def chip_body(passing, me, c, x, keep_ref, far_ref, near_ref, send_ref):
        base = head0 + c * half
        for part, to in ((x, near_ref), (1 - x, send_ref)):
            for i in range(quarter):
                h = part * quarter + i
                fade = passing[me | 1, base + h]
                a, b = jnp.where(c == 0, fade, 1.0), jnp.where(c == 0, 1.0, fade)
                to[i] = (keep_ref[h] * a + far_ref[h] * b).astype(to.dtype)

    def plane_body(passing, me, c, x, near_ref, far_ref, out_ref):
        base = head0 + c * half + x * quarter
        for i in range(quarter):
            fade = passing[me | 3, base + i] * passing[(me | 3) - 1, base + i]
            a, b = jnp.where(x == 0, fade, 1.0), jnp.where(x == 0, 1.0, fade)
            out_ref[i] = (near_ref[i] * a + far_ref[i].astype(F32) * b).astype(BF16)

    def enter_body(passing, me, c, x, near_ref, far_ref, one_ref, two_ref, keep_ref, send_ref):
        base = head0 + c * half + x * quarter
        plane = me & ~3
        low = jnp.maximum(plane - 4, 0)
        for i in range(quarter):
            h = base + i
            fade = passing[low, h] * passing[low + 1, h] * passing[low + 2, h] * passing[low + 3, h]
            e0 = jnp.where(me >= 4, one_ref[i].astype(F32), 0.0)
            e0 = jnp.where(me >= 8, e0 + two_ref[i].astype(F32) * fade, e0)
            chip = jnp.where(x == 0, near_ref[i], far_ref[i].astype(F32))
            e1 = e0 * (passing[plane, h] * passing[plane + 1, h]) + chip
            keep_ref[i] = jnp.where(x == 0, e0, e1)
            send_ref[i] = jnp.where(x == 0, e1, e0).astype(BF16)

    def core_body(passing, me, c, x, keep_ref, far_ref, near_ref, got_ref, mine_ref, send_ref):
        base = head0 + c * half
        mine_on, other_on = passing[me, heads], passing[me ^ 1, heads]
        for part, source in ((x, near_ref), (1 - x, got_ref)):
            for i in range(quarter):
                h = part * quarter + i
                e0 = source[i].astype(F32)
                first = jnp.where(c == 0, keep_ref[h], far_ref[h])
                e1 = e0 * passing[me & ~1, base + h] + first
                mine_ref[h] = (jnp.where(c == 0, e0, e1) * mine_on).astype(BF16)
                send_ref[h] = (jnp.where(c == 0, e1, e0) * other_on).astype(BF16)

    sent = moved(send, core(shards))
    near_q, send_q = mixing(
        "mix_chip", chip_body, passing, place, [keep, sent], [(quarter, F32), (quarter, BF16)]
    )
    far_q = moved(send_q, cross(shards))
    wait = yield send_q
    near_q = near_q if wait is None else after(near_q, wait)
    (plane_state,) = mixing(
        "mix_plane", plane_body, passing, place, [near_q, far_q], [(quarter, BF16)]
    )
    one_below = moved(plane_state, up(shards))
    yield plane_state, one_below
    two_below = moved(one_below, up(shards))
    wait = yield two_below
    near_q = near_q if wait is None else after(near_q, wait)
    near_e, send_e = mixing(
        "mix_enter",
        enter_body,
        passing,
        place,
        [near_q, far_q, one_below, two_below],
        [(quarter, F32), (quarter, BF16)],
    )
    got_e = moved(send_e, cross(shards))
    yield got_e
    mine, other = mixing(
        "mix_core", core_body, passing, place, [keep, sent, near_e, got_e], [(half, BF16), (half, BF16)]
    )
    yield mine, moved(other, core(shards))


def carried_in_any(state, passing, me, shards):
    states = lax.all_gather(state, "seq")

    def turn(j, total):
        part = passing[j][:, None, None] * total + states[j].astype(F32)
        return jnp.where(j < me, part, total)

    return lax.fori_loop(0, shards, turn, jnp.zeros(state.shape, F32)).astype(BF16)


def body(
    sparse_query, sparse_key, sparse_value, light_query, light_key, log_decay, segments, block_list
):
    tokens = sparse_query.shape[0]
    kv_heads = sparse_key.shape[1] // HD
    heads = light_query.shape[1] // HD
    group = heads // kv_heads
    shards = lax.axis_size("seq")
    me = lax.axis_index("seq")
    place = me.astype(jnp.int32).reshape(1)
    planes = shards == 16 and kv_heads == 4
    chunks = 2 if planes else 1
    kv_chunk = kv_heads // chunks
    head_chunk = heads // chunks
    parts = []
    for chunk in range(chunks):
        cols = slice(chunk * kv_chunk * HD, (chunk + 1) * kv_chunk * HD)
        parts += [sparse_key[:, cols], sparse_value[:, cols]]
    own = jnp.concatenate(parts, axis=1)
    seg_col, seg_row, listing = segments[:, None], segments[None, :], block_list.reshape(-1)
    if planes:
        beside = moved(own, cross(shards))
        below = moved(own, up(shards))
    else:
        pieces = [lax.all_gather(own, "seq", axis=0, tiled=True)]
    whiches = []
    for chunk in range(chunks):
        turns = [1 - (me & 1), me & 1] if planes else range(kv_chunk)
        for kv_head in turns:
            kv_head = jnp.asarray(kv_head, jnp.int32)
            at = [chunk * kv_chunk + kv_head, chunk * 2 * kv_chunk + kv_head]
            whiches.append(jnp.stack(at))
    order = jnp.stack([which[0] for which in whiches])
    info = own_info(log_decay, seg_row, shards)
    info, whiches, order, place, listing, seg_col = after(
        (info, whiches, order, place, listing, seg_col), own
    )
    known = lax.all_to_all(info, "seq", 0, 0, tiled=True)
    passing = all_passing(known, heads, tokens)
    sizes = (1,) * 11 if planes else (shards,)
    *biases, table = seen_table(place, listing, known, seg_col, seg_row, sizes, heads, planes)
    if planes:
        beside, below = after((beside, below), known)
        below_beside = moved(below, cross(shards))
        second = moved(below, up(shards))
        own_far, below_far, beside_far = (
            moved(part, core(shards)) for part in (own, below, beside)
        )
        light_query, light_key = after((light_query, light_key), table)
    weights, faded_k, faded_q = local_part(
        light_query, light_key, log_decay, seg_col, seg_row, group
    )
    if planes:
        below_beside, second, weights, faded_k, faded_q = after(
            (below_beside, second, weights, faded_k, faded_q)
        )
        span = own.shape[1] // 2
        lasts = [moved(below_beside[:, span:], up(shards))]
        lasts.insert(0, moved(second[:, :span], cross(shards)))
        second_far, below_beside_far = (
            moved(part, core(shards)) for part in (second, below_beside)
        )
        last_fars = [moved(last, core(shards)) for last in lasts]
        pieces = [below, second, beside, below_beside, lasts, own_far, below_far, second_far]
        pieces += [beside_far, below_beside_far, last_fars]

    def attend(turn, first=None):
        which = whiches[turn] if first is None else after(whiches[turn], first)
        chunk = turn // kv_chunk
        mine = [p[chunk] if isinstance(p, list) else p for p in pieces]
        shifts = [chunk * 2 * kv_chunk if isinstance(p, list) else 0 for p in pieces]
        return attend_part(
            which, table, biases, sparse_query, own, faded_k, mine, sizes, shifts, kv_chunk
        )

    if planes:
        part0, send0 = attend(0)
        part1, keep0 = attend(1, part0)
        carry0 = carried_in_planes(keep0, send0, passing, place, shards, 0, heads)
        part2, send1 = attend(2, next(carry0))
        plane0, one0 = next(carry0)
        part3, keep1 = attend(3, (part2, plane0))
        next(carry0)
        keep1 = after(keep1, one0)
        carry1 = carried_in_planes(keep1, send1, passing, place, shards, head_chunk, heads)
        order = after(order, next(carry1))
        inside, attended = inside_part(order, weights, [part0, part1, part2, part3])
        got0 = next(carry0)
        carry1.send(inside)
        next(carry1)
        carry1.send(got0)
        states = [next(carry0), next(carry1)]
    else:
        parts, found = zip(*[attend(turn) for turn in range(kv_heads)], strict=True)
        inside, attended = inside_part(order, weights, parts)
        entering = carried_in_any(jnp.concatenate(found), passing[:, :heads], me, shards)
        entering = entering * passing[me, heads].astype(BF16)
        states = [(entering, entering)]
    result, squares = output_part(place, inside, faded_q, states, group, planes)
    if lax.axis_size("head") == 2:
        squares = squares + lax.ppermute(squares, "head", [(0, 1), (1, 0)])
    else:
        squares = lax.psum(squares, "head")
    return (attended, scale_part(squares, result, 8))


def solution(mesh):
    in_specs = (
        P("seq", "head"),
        P("seq", "head"),
        P("seq", "head"),
        P("seq", "head"),
        P("seq", "head"),
        P("head", "seq"),
        P("seq"),
        P("seq", None),
    )
    out_specs = (P("seq", "head"), P("seq", "head"))
    return jax.shard_map(body, mesh=mesh, in_specs=in_specs, out_specs=out_specs, check_vma=False)
```
